128 devices in a mesh: ctx: 32 (over z, x_hi, y), tp: 4 (over x_lo, core).
Axes of the slice: x: 4 (x_hi: 2, x_lo: 2; x = x_hi * 2 + x_lo), y: 4, z: 4, core: 2. Of those that a mesh axis runs over, the one named last changes fastest.
Arguments:
- queries: bfloat16 [16384, 4096], P('ctx', 'tp'), may hold values from -6 to 6
- keys: bfloat16 [16384, 512], P('ctx', 'tp'), may hold values from -6 to 6
- values: bfloat16 [16384, 512], P('ctx', 'tp'), may hold values from -6 to 6
- out_weight: bfloat16 [4096, 8192], P('tp'), may hold values from -0.75 to 0.75
- vertical: int32 [32, 16], P('tp'), may hold values from 0 to 255, as said below
- slash: int32 [32, 8], P('tp'), may hold values from 0 to 15, as said below
Outputs:
- projected: bfloat16 [16384, 8192], P(('ctx', 'tp'))
The draws below stay inside these ranges and needn't reach their ends.
Inputs may be any that keep to these rules, and one draw needn't show every extreme that they name: `vertical`: each head's 16 blocks are distinct. For each index of tp, the blocks named by its 8 heads include at most 2 blocks of any one ctx shard of 512 tokens, and exactly 2 of some shard. `slash`: each head's first offset is 0 and its 8 offsets are distinct.
All inputs are finite; a program needn't handle non-finite values.
Results may differ from the reference program's by a relative error of at most 0.013.
Values may be sent and summed in bfloat16 or wider, within the bound.
A program may use at most 128 MiB of HBM per device.

```python
import jax
import jax.numpy as jnp
from jax import lax

D = 8192
QH = 32
KVH = 4
HS = 128
BLK = 64
NV = 16
NS = 8
VMOST = 2
TOKENS = 16384
BLK_DEV = 8
SPAN = 16
HEADS_DEV = 8
POOL = 64


def draw_keys(key, part):
    shape_full = (TOKENS, KVH * HS)
    result = jax.random.truncated_normal(jax.random.fold_in(key, 31), -6.0, 6.0, shape_full, jnp.float32)
    return result.astype(jnp.bfloat16)


def draw_queries(key, part):
    shape_full = (TOKENS, QH * HS)
    result = jax.random.truncated_normal(jax.random.fold_in(key, 21), -6.0, 6.0, shape_full, jnp.float32)
    return result.astype(jnp.bfloat16)


def draw_vertical(key, part):
    shard_count = POOL // VMOST
    groups = QH // HEADS_DEV
    local_scores = jax.random.randint(jax.random.fold_in(key, 3), (groups, shard_count, BLK_DEV), 0, 65536) * BLK_DEV + jnp.arange(BLK_DEV, dtype=jnp.int32)
    local_order = jnp.argsort(local_scores, axis=-1, stable=True)[:, :, :VMOST]
    pool_blocks = (jnp.arange(shard_count, dtype=jnp.int32)[None, :, None] * BLK_DEV + local_order).reshape(groups, POOL)
    pool_owner = jnp.arange(POOL, dtype=jnp.int32) // VMOST
    favored = jax.random.randint(jax.random.fold_in(key, 5), (groups,), 0, shard_count)
    pool_ids = jnp.arange(POOL, dtype=jnp.int32)
    head_scores = jax.random.randint(jax.random.fold_in(key, 9), (groups, HEADS_DEV, POOL), 0, 65536) * POOL + pool_ids
    first_head = jnp.arange(HEADS_DEV)[None, :, None] == 0
    forced = first_head & (pool_owner[None, None, :] == favored[:, None, None])
    head_scores = jnp.where(forced, pool_ids - POOL, head_scores)
    chosen = jnp.argsort(head_scores, axis=-1, stable=True)[:, :, :NV]
    picked = jnp.take_along_axis(jnp.broadcast_to(pool_blocks[:, None, :], (groups, HEADS_DEV, POOL)), chosen, axis=-1)
    return picked.reshape(QH, NV).astype(jnp.int32)


def draw_slash(key, part):
    row_keys = jax.random.split(jax.random.fold_in(key, 4), QH)

    def one_row(row_key):
        shuffled = jax.random.permutation(row_key, SPAN - 1) + 1
        return jnp.concatenate([jnp.zeros((1,), jnp.int32), shuffled[:NS - 1].astype(jnp.int32)])
    return jax.vmap(one_row)(row_keys).astype(jnp.int32)


def level_of(stream_key, shape, cuts, smallest, high):
    def one(axis_at, shards_of):
        draws = jax.random.uniform(jax.random.fold_in(jax.random.fold_in(stream_key, 6), axis_at), (shards_of,), jnp.float32, smallest / len(cuts), high / len(cuts))
        return jnp.repeat(jnp.exp(draws), shape[axis_at] // shards_of).reshape((-1,) + (1,) * (len(shape) - axis_at - 1))

    factor_of = one(*cuts[0])
    for cut in cuts[1:]:
        factor_of = factor_of * one(*cut)
    return factor_of


def scatter_about(rng, extent, deviation, reach, cuts=(), held_as=jnp.bfloat16):
    drawn = jax.random.normal(rng, extent, jnp.float32) * deviation
    if len(cuts) > 0:
        drawn = level_of(rng, extent, cuts, -0.22, 0.18) * drawn
    return jnp.clip(drawn, min=-reach, max=reach).astype(held_as)


def setup_inputs(seed: int = 0) -> dict:
    key_of = jax.random.split(jax.random.key(seed), 7)
    return {
        "queries": draw_queries(jax.random.fold_in(key_of[6], 71), 0),
        "keys": draw_keys(jax.random.fold_in(key_of[6], 71), 0),
        "values": scatter_about(key_of[2], (TOKENS, KVH * HS), 1.0, 6.0, ((0, 32), (1, 4))),
        "out_weight": scatter_about(key_of[3], (QH * HS, D), 64 ** -0.5, 0.75, ((0, 4),)),
        "vertical": draw_vertical(jax.random.fold_in(key_of[6], 71), 0),
        "slash": draw_slash(jax.random.fold_in(key_of[6], 71), 0),
    }


def slot_table(vert_row, slash_row, query_blocks):
    block_count = query_blocks.shape[0]
    column_ids = query_blocks[:, None]
    vert_blocks = jnp.broadcast_to(vert_row[None, :], (block_count, vert_row.shape[0]))
    vert_ok = vert_blocks <= column_ids
    slash_blocks = column_ids - slash_row[None, :]
    repeated = jnp.any(slash_blocks[:, :, None] == vert_row[None, None, :], axis=2)
    slash_ok = (slash_blocks >= 0) & jnp.logical_not(repeated)
    blocks = jnp.concatenate([vert_blocks, slash_blocks], axis=1).astype(jnp.int32)
    usable = jnp.concatenate([vert_ok, slash_ok], axis=1)
    return (blocks, usable)

def attend_ref(head_query, key_tiles, value_tiles, blocks, usable, query_blocks):
    block_len = head_query.shape[1]
    score_scale = 1.0 / jnp.sqrt(jnp.float32(head_query.shape[2]))
    scores = jnp.einsum('ibd,isjd->ibsj', head_query.astype(jnp.float32), key_tiles.astype(jnp.float32)) * score_scale
    diagonal = blocks == query_blocks[:, None]
    positions = jnp.arange(block_len, dtype=jnp.int32)
    above_diag = positions[None, :] > positions[:, None]
    blocked = jnp.logical_not(usable)[:, None, :, None] | diagonal[:, None, :, None] & above_diag[None, :, None, :]
    scores = jnp.where(blocked, jnp.float32(-1e+30), scores)
    row_max = lax.optimization_barrier(jnp.max(scores, axis=(2, 3), keepdims=True))
    weights = jnp.exp(scores - row_max)
    row_total = lax.optimization_barrier(jnp.sum(weights, axis=(2, 3)))
    rounded_probs = weights.astype(jnp.bfloat16)
    attended = jnp.einsum('ibsj,isjd->ibd', rounded_probs.astype(jnp.float32), value_tiles.astype(jnp.float32))
    return (attended / row_total[:, :, None]).astype(jnp.bfloat16)

def reference(queries, keys, values, out_weight, vertical, slash):
    total_blocks = TOKENS // BLK
    group_size = QH // KVH
    query_blocks = jnp.arange(total_blocks, dtype=jnp.int32)

    def one_head(head_index):
        kv_index = head_index // group_size
        key_head = lax.dynamic_slice_in_dim(keys, kv_index * HS, HS, 1).reshape(total_blocks, BLK, HS)
        value_head = lax.dynamic_slice_in_dim(values, kv_index * HS, HS, 1).reshape(total_blocks, BLK, HS)
        head_query = lax.dynamic_slice_in_dim(queries, head_index * HS, HS, 1).reshape(total_blocks, BLK, HS)
        blocks, usable = slot_table(vertical[head_index], slash[head_index], query_blocks)
        clipped = jnp.clip(blocks, 0, total_blocks - 1)
        return attend_ref(head_query, key_head[clipped], value_head[clipped], blocks, usable, query_blocks)
    heads_out = lax.map(one_head, jnp.arange(QH, dtype=jnp.int32))
    attended = heads_out.transpose(1, 2, 0, 3).reshape(TOKENS, QH * HS)
    width = HEADS_DEV * HS
    summed = jnp.zeros((TOKENS, D), jnp.float32)
    for group_index in range(QH // HEADS_DEV):
        product = jnp.dot(attended[:, group_index * width:(group_index + 1) * width], out_weight[group_index * width:(group_index + 1) * width], preferred_element_type=jnp.float32)
        rounded = lax.optimization_barrier(product.astype(jnp.bfloat16))
        summed = summed + rounded.astype(jnp.float32)
    return summed.astype(jnp.bfloat16)
```

```python
import functools

import jax
import jax.numpy as jnp
from jax import lax
from jax.experimental import pallas as pl
from jax.experimental.pallas import tpu as pltpu
from jax.sharding import PartitionSpec as P

HS = 128
BLK = 64
NEG = -1e30


def attend_kernel(slots, slash, q_ref, kp_ref, vp_ref, kw_ref, vw_ref, bv_ref, bs_ref, o_ref):
    h = pl.program_id(0)
    local_blocks = q_ref.shape[0] // BLK
    nv, ns = slots.shape[1], slash.shape[1]
    reach = kw_ref.shape[0] // BLK - local_blocks
    scale = 1.0 / (HS**0.5)
    k_vert = jnp.concatenate(
        [kp_ref[pl.ds(pl.multiple_of(slots[h, j] * BLK, BLK), BLK), :] for j in range(nv)], axis=0
    )
    v_vert = jnp.concatenate(
        [vp_ref[pl.ds(pl.multiple_of(slots[h, j] * BLK, BLK), BLK), :] for j in range(nv)], axis=0
    )
    row = lax.broadcasted_iota(jnp.int32, (BLK, BLK), 0)
    col = lax.broadcasted_iota(jnp.int32, (BLK, BLK), 1)
    triangle = jnp.where(col > row, NEG, 0.0).astype(jnp.float32)
    triangle = jnp.concatenate([triangle, jnp.zeros((BLK, (ns - 1) * BLK), jnp.float32)], axis=1)
    for pair in range(local_blocks // 2):
        q = q_ref[pl.ds(pair * 2 * BLK, 2 * BLK), :]
        s_vert = lax.dot_general(
            q, k_vert, (((1,), (1,)), ((), ())), preferred_element_type=jnp.float32
        )
        probs, outs, totals = [], [], []
        for half in range(2):
            i = 2 * pair + half
            at = [pl.multiple_of((reach + i - slash[h, j]) * BLK, BLK) for j in range(ns)]
            k_s = jnp.concatenate([kw_ref[pl.ds(a, BLK), :] for a in at], axis=0)
            v_s = jnp.concatenate([vw_ref[pl.ds(a, BLK), :] for a in at], axis=0)
            qi = q[half * BLK : (half + 1) * BLK]
            s_s = lax.dot_general(
                qi, k_s, (((1,), (1,)), ((), ())), preferred_element_type=jnp.float32
            )
            s_s = s_s * scale + (bs_ref[0, pl.ds(i, 1), :] + triangle)
            s_v = s_vert[half * BLK : (half + 1) * BLK] * scale + bv_ref[0, pl.ds(i, 1), :]
            m = jnp.maximum(
                jnp.max(s_v, axis=1, keepdims=True), jnp.max(s_s, axis=1, keepdims=True)
            )
            w_v = jnp.exp(s_v - m)
            w_s = jnp.exp(s_s - m)
            totals.append(
                jnp.sum(w_v, axis=1, keepdims=True) + jnp.sum(w_s, axis=1, keepdims=True)
            )
            probs.append(w_v.astype(jnp.bfloat16))
            outs.append(
                jnp.dot(w_s.astype(jnp.bfloat16), v_s, preferred_element_type=jnp.float32)
            )
        o_v = jnp.dot(
            jnp.concatenate(probs, axis=0), v_vert, preferred_element_type=jnp.float32
        )
        o = (o_v + jnp.concatenate(outs, axis=0)) / jnp.concatenate(totals, axis=0)
        o_ref[pl.ds(pair * 2 * BLK, 2 * BLK), :] = o.astype(jnp.bfloat16)


def shards(ctx_size, queries, keys, values, out_weight, vertical, slash):
    rows, width = queries.shape
    heads, nv = vertical.shape
    ns = slash.shape[1]
    blocks = rows // BLK
    me = lax.axis_index("ctx")
    first = me * blocks

    flat = vertical.reshape(-1)
    mine = flat // blocks == me
    inside = flat % blocks
    low = jnp.min(jnp.where(mine, inside, blocks - 1))
    high = jnp.max(jnp.where(mine, inside, 0))
    kv = jnp.concatenate([keys, values], axis=1)
    picked = jnp.concatenate(
        [
            lax.dynamic_slice_in_dim(kv, low * BLK, BLK, 0),
            lax.dynamic_slice_in_dim(kv, high * BLK, BLK, 0),
        ],
        axis=0,
    )
    pool = lax.all_gather(picked, "ctx", axis=0, tiled=True)
    back1 = lax.ppermute(kv, "ctx", [(i, i + 1) for i in range(ctx_size - 1)])
    back2 = lax.ppermute(kv, "ctx", [(i, i + 2) for i in range(ctx_size - 2)])
    window = jnp.concatenate([back2, back1, kv], axis=0)

    second = jnp.any(
        (flat[:, None] // blocks == flat[None, :] // blocks) & (flat[None, :] < flat[:, None]),
        axis=1,
    )
    slots = (2 * (flat // blocks) + second.astype(jnp.int32)).reshape(heads, nv)
    query_blocks = first + jnp.arange(blocks, dtype=jnp.int32)
    away = query_blocks[None, :, None] - vertical[:, None, :]
    repeated = jnp.any(away[..., None] == slash[:, None, None, :], axis=-1)
    bias_v = jnp.where((away > 0) & ~repeated, 0.0, NEG).astype(jnp.float32)
    bias_s = jnp.where(query_blocks[None, :, None] >= slash[:, None, :], 0.0, NEG)
    bias_v = jnp.broadcast_to(bias_v[..., None], (heads, blocks, nv, BLK)).reshape(
        heads, blocks, nv * BLK
    )
    bias_s = jnp.broadcast_to(
        bias_s.astype(jnp.float32)[..., None], (heads, blocks, ns, BLK)
    ).reshape(heads, blocks, ns * BLK)

    whole = lambda n: pl.BlockSpec((n, HS), lambda h, *_: (0, 0))
    attended = pl.pallas_call(
        attend_kernel,
        out_shape=jax.ShapeDtypeStruct((rows, width), jnp.bfloat16),
        grid_spec=pltpu.PrefetchScalarGridSpec(
            num_scalar_prefetch=2,
            grid=(heads,),
            in_specs=[
                pl.BlockSpec((rows, HS), lambda h, *_: (0, h)),
                pl.BlockSpec((pool.shape[0], HS), lambda h, *_: (0, 0)),
                pl.BlockSpec((pool.shape[0], HS), lambda h, *_: (0, 1)),
                pl.BlockSpec((window.shape[0], HS), lambda h, *_: (0, 0)),
                pl.BlockSpec((window.shape[0], HS), lambda h, *_: (0, 1)),
                pl.BlockSpec((1, blocks, nv * BLK), lambda h, *_: (h, 0, 0)),
                pl.BlockSpec((1, blocks, ns * BLK), lambda h, *_: (h, 0, 0)),
            ],
            out_specs=pl.BlockSpec((rows, HS), lambda h, *_: (0, h)),
        ),
        compiler_params=pltpu.CompilerParams(vmem_limit_bytes=48 << 20),
    )(slots, slash, queries, pool, pool, window, window, bias_v, bias_s)
    product = jnp.dot(attended, out_weight, preferred_element_type=jnp.float32)
    return lax.psum_scatter(
        product.astype(jnp.bfloat16), "tp", scatter_dimension=0, tiled=True
    )


def solution(mesh):
    return jax.shard_map(
        functools.partial(shards, mesh.shape["ctx"]),
        mesh=mesh,
        in_specs=(
            P("ctx", "tp"),
            P("ctx", "tp"),
            P("ctx", "tp"),
            P("tp", None),
            P("tp", None),
            P("tp", None),
        ),
        out_specs=P(("ctx", "tp"), None),
        check_vma=False,
    )
```

```python
import functools

import jax
import jax.numpy as jnp
from jax import lax
from jax.experimental import pallas as pl
from jax.experimental.pallas import tpu as pltpu
from jax.sharding import PartitionSpec as P

HS = 128
BLK = 64
NEG = -1e30


MESH = pl.DeviceIdType.MESH
WIDE = 1024


def attend_head(h, base, slots, slash, q_ref, kp_ref, kw_ref, bv_ref, bs_ref, att_ref):
    nv, ns = slots.shape[1], slash.shape[1]
    local_blocks = q_ref.shape[0] // BLK
    reach = kw_ref.shape[0] - local_blocks
    scale = 1.0 / (HS**0.5)
    lanes = pl.ds(pl.multiple_of(h * HS, HS), HS)
    at_v = [slots[h, j] for j in range(nv)]
    k_vert = jnp.concatenate([kp_ref[a, :, :HS] for a in at_v], axis=0)
    v_vert = jnp.concatenate([kp_ref[a, :, HS:] for a in at_v], axis=0)
    row = lax.broadcasted_iota(jnp.int32, (BLK, BLK), 0)
    col = lax.broadcasted_iota(jnp.int32, (BLK, BLK), 1)
    triangle = jnp.where(col > row, NEG, 0.0).astype(jnp.float32)
    triangle = jnp.concatenate([triangle, jnp.zeros((BLK, (ns - 1) * BLK), jnp.float32)], axis=1)
    q = q_ref[pl.ds(pl.multiple_of(base * BLK, BLK), 2 * BLK), lanes]
    s_vert = lax.dot_general(
        q, k_vert, (((1,), (1,)), ((), ())), preferred_element_type=jnp.float32
    )
    probs, outs, totals = [], [], []
    for half in range(2):
        i = base + half
        at = [reach + i - slash[h, j] for j in range(ns)]
        k_s = jnp.concatenate([kw_ref[a, :, :HS] for a in at], axis=0)
        v_s = jnp.concatenate([kw_ref[a, :, HS:] for a in at], axis=0)
        qi = q[half * BLK : (half + 1) * BLK]
        s_s = lax.dot_general(
            qi, k_s, (((1,), (1,)), ((), ())), preferred_element_type=jnp.float32
        )
        s_s = s_s * scale + (bs_ref[h, pl.ds(i, 1), :] + triangle)
        s_v = s_vert[half * BLK : (half + 1) * BLK] * scale + bv_ref[h, pl.ds(i, 1), :]
        m = jnp.maximum(jnp.max(s_v, axis=1, keepdims=True), jnp.max(s_s, axis=1, keepdims=True))
        w_v = jnp.exp(s_v - m)
        w_s = jnp.exp(s_s - m)
        totals.append(jnp.sum(w_v, axis=1, keepdims=True) + jnp.sum(w_s, axis=1, keepdims=True))
        probs.append(w_v.astype(jnp.bfloat16))
        outs.append(jnp.dot(w_s.astype(jnp.bfloat16), v_s, preferred_element_type=jnp.float32))
    o_v = jnp.dot(jnp.concatenate(probs, axis=0), v_vert, preferred_element_type=jnp.float32)
    o = (o_v + jnp.concatenate(outs, axis=0)) / jnp.concatenate(totals, axis=0)
    att_ref[:, lanes] = o.astype(jnp.bfloat16)


def layer_kernel(
    slots, slash, q_ref, kp_ref, kw_ref, bv_ref, bs_ref, w_hbm, out_ref,
    att, w, to_sib, from_sib, to_cross, from_cross,
    w_sem, sib_send, sib_recv, cross_send, cross_recv,
):
    heads = slots.shape[0]
    chunks = w.shape[0]
    quarter = out_ref.shape[0] // BLK
    t = lax.axis_index("tp")
    chip, core = t // 2, t % 2
    sibling = 2 * chip + (1 - core)
    cross = 2 * (1 - chip) + core

    barrier = pltpu.get_barrier_semaphore()
    for other in (sibling, cross):
        pl.semaphore_signal(barrier, inc=1, device_id={"tp": other}, device_id_type=MESH)

    def weights(c):
        at = pl.ds(pl.multiple_of(c * WIDE, WIDE), WIDE)
        return pltpu.make_async_copy(w_hbm.at[:, at], w.at[c], w_sem.at[c])

    def hand(k, c):
        return pltpu.make_async_remote_copy(
            src_ref=to_sib.at[k, c],
            dst_ref=from_sib.at[k, c],
            send_sem=sib_send.at[k, c],
            recv_sem=sib_recv.at[k, c],
            device_id={"tp": sibling},
            device_id_type=MESH,
        )

    def over(c):
        return pltpu.make_async_remote_copy(
            src_ref=to_cross.at[c],
            dst_ref=from_cross.at[c],
            send_sem=cross_send.at[c],
            recv_sem=cross_recv.at[c],
            device_id={"tp": cross},
            device_id_type=MESH,
        )

    @pl.loop(0, chunks)
    def _(c):
        weights(c).start()

    pl.semaphore_wait(barrier, 2)

    @pl.loop(0, 4)
    def _(stage):
        there, swap = 1 - stage // 2, 1 - stage % 2
        owner = 2 * (chip + (1 - 2 * chip) * there) + core + (1 - 2 * core) * swap

        @pl.loop(0, heads)
        def _(h):
            attend_head(h, owner * quarter, slots, slash, q_ref, kp_ref, kw_ref, bv_ref, bs_ref, att)

        @pl.loop(0, chunks)
        def _(c):
            @pl.when(stage == 0)
            def _():
                weights(c).wait()

            y = jnp.dot(att[...], w[c], preferred_element_type=jnp.float32)

            @pl.when(stage == 0)
            def _():
                to_sib[0, c] = y.astype(jnp.bfloat16)
                hand(0, c).start()

            @pl.when(stage == 1)
            def _():
                hand(0, c).wait_recv()
                to_cross[c] = (y + from_sib[0, c].astype(jnp.float32)).astype(jnp.bfloat16)
                over(c).start()

            @pl.when(stage == 2)
            def _():
                to_sib[1, c] = y.astype(jnp.bfloat16)
                hand(1, c).start()

            @pl.when(stage == 3)
            def _():
                hand(1, c).wait_recv()
                over(c).wait_recv()
                at = pl.ds(pl.multiple_of(c * WIDE, WIDE), WIDE)
                out_ref[:, at] = (
                    y + from_sib[1, c].astype(jnp.float32) + from_cross[c].astype(jnp.float32)
                ).astype(jnp.bfloat16)

    @pl.loop(0, chunks)
    def _(c):
        hand(0, c).wait_send()
        hand(1, c).wait_send()
        over(c).wait_send()


def shards(ctx_size, queries, keys, values, out_weight, vertical, slash):
    rows, width = queries.shape
    heads, nv = vertical.shape
    ns = slash.shape[1]
    blocks = rows // BLK
    me = lax.axis_index("ctx")
    first = me * blocks

    flat = vertical.reshape(-1)
    mine = flat // blocks == me
    inside = flat % blocks
    low = jnp.min(jnp.where(mine, inside, blocks - 1))
    high = jnp.max(jnp.where(mine, inside, 0))
    kv = jnp.concatenate([keys, values], axis=1)
    picked = jnp.concatenate(
        [
            lax.dynamic_slice_in_dim(kv, low * BLK, BLK, 0),
            lax.dynamic_slice_in_dim(kv, high * BLK, BLK, 0),
        ],
        axis=0,
    )
    pool = lax.all_gather(picked, "ctx", axis=0, tiled=True)
    back1 = lax.ppermute(kv, "ctx", [(i, i + 1) for i in range(ctx_size - 1)])
    back2 = lax.ppermute(kv, "ctx", [(i, i + 2) for i in range(ctx_size - 2)])
    window = jnp.concatenate([back2, back1, kv], axis=0)

    second = jnp.any(
        (flat[:, None] // blocks == flat[None, :] // blocks) & (flat[None, :] < flat[:, None]),
        axis=1,
    )
    slots = (2 * (flat // blocks) + second.astype(jnp.int32)).reshape(heads, nv)
    query_blocks = first + jnp.arange(blocks, dtype=jnp.int32)
    away = query_blocks[None, :, None] - vertical[:, None, :]
    repeated = jnp.any(away[..., None] == slash[:, None, None, :], axis=-1)
    bias_v = jnp.where((away > 0) & ~repeated, 0.0, NEG).astype(jnp.float32)
    bias_s = jnp.where(query_blocks[None, :, None] >= slash[:, None, :], 0.0, NEG)
    bias_v = jnp.broadcast_to(bias_v[..., None], (heads, blocks, nv, BLK)).reshape(
        heads, blocks, nv * BLK
    )
    bias_s = jnp.broadcast_to(
        bias_s.astype(jnp.float32)[..., None], (heads, blocks, ns, BLK)
    ).reshape(heads, blocks, ns * BLK)

    chunks = out_weight.shape[1] // WIDE
    part = (rows // 4, WIDE)
    vmem = pl.BlockSpec(memory_space=pltpu.VMEM)
    smem = pl.BlockSpec(memory_space=pltpu.SMEM)
    return pl.pallas_call(
        layer_kernel,
        out_shape=jax.ShapeDtypeStruct((rows // 4, out_weight.shape[1]), jnp.bfloat16),
        in_specs=[smem, smem, vmem, vmem, vmem, vmem, vmem, pl.BlockSpec(memory_space=pl.ANY)],
        out_specs=vmem,
        scratch_shapes=[
            pltpu.VMEM((rows // 4, width), jnp.bfloat16),
            pltpu.VMEM((chunks, width, WIDE), jnp.bfloat16),
            pltpu.VMEM((2, chunks) + part, jnp.bfloat16),
            pltpu.VMEM((2, chunks) + part, jnp.bfloat16),
            pltpu.VMEM((chunks,) + part, jnp.bfloat16),
            pltpu.VMEM((chunks,) + part, jnp.bfloat16),
            pltpu.SemaphoreType.DMA((chunks,)),
            pltpu.SemaphoreType.DMA((2, chunks)),
            pltpu.SemaphoreType.DMA((2, chunks)),
            pltpu.SemaphoreType.DMA((chunks,)),
            pltpu.SemaphoreType.DMA((chunks,)),
        ],
        compiler_params=pltpu.CompilerParams(
            collective_id=0, has_side_effects=True, vmem_limit_bytes=52 << 20
        ),
    )(
        slots, slash, queries, pool.reshape(-1, BLK, 2 * HS), window.reshape(-1, BLK, 2 * HS),
        bias_v, bias_s, out_weight,
    )


def solution(mesh):
    return jax.shard_map(
        functools.partial(shards, mesh.shape["ctx"]),
        mesh=mesh,
        in_specs=(
            P("ctx", "tp"),
            P("ctx", "tp"),
            P("ctx", "tp"),
            P("tp", None),
            P("tp", None),
            P("tp", None),
        ),
        out_specs=P(("ctx", "tp"), None),
        check_vma=False,
    )
```

```python
import jax
import jax.numpy as jnp
from jax import lax
from jax.experimental import pallas as pl
from jax.experimental.pallas import tpu as pltpu
from jax.sharding import PartitionSpec as P

HS = 128
BLK = 64
NEG = -1e30
MESH = pl.DeviceIdType.MESH
WIDE = 1024
NZ, NX, NY = 4, 2, 4


def attend_head(h, base, slots, vertical, slash, q_ref, pool, window, bv, bs, att):
    nv, ns = vertical.shape[1], slash.shape[1]
    reach = window.shape[0] - q_ref.shape[0] // BLK
    scale = 1.0 / (HS**0.5)
    lanes = pl.ds(pl.multiple_of(h * HS, HS), HS)
    at_v = []
    for j in range(nv):
        s = vertical[h, j] // 8
        at_v.append((s // (NX * NY), (s // NY) % NX, s % NY, slots[h, j]))
    k_vert = jnp.concatenate([pool[a, b, c, d, :, :HS] for a, b, c, d in at_v], axis=0)
    v_vert = jnp.concatenate([pool[a, b, c, d, :, HS:] for a, b, c, d in at_v], axis=0)
    row = lax.broadcasted_iota(jnp.int32, (BLK, BLK), 0)
    col = lax.broadcasted_iota(jnp.int32, (BLK, BLK), 1)
    triangle = jnp.where(col > row, NEG, 0.0).astype(jnp.float32)
    triangle = jnp.concatenate([triangle, jnp.zeros((BLK, (ns - 1) * BLK), jnp.float32)], axis=1)
    q = q_ref[pl.ds(pl.multiple_of(base * BLK, BLK), 2 * BLK), lanes]
    s_vert = lax.dot_general(
        q, k_vert, (((1,), (1,)), ((), ())), preferred_element_type=jnp.float32
    )
    probs, outs, totals = [], [], []
    for half in range(2):
        i = base + half
        at = [reach + i - slash[h, j] for j in range(ns)]
        k_s = jnp.concatenate([window[a, :, :HS] for a in at], axis=0)
        v_s = jnp.concatenate([window[a, :, HS:] for a in at], axis=0)
        qi = q[half * BLK : (half + 1) * BLK]
        s_s = lax.dot_general(
            qi, k_s, (((1,), (1,)), ((), ())), preferred_element_type=jnp.float32
        )
        s_s = s_s * scale + (bs[i, pl.ds(h, 1), :] + triangle)
        s_v = s_vert[half * BLK : (half + 1) * BLK] * scale + bv[i, pl.ds(h, 1), :]
        m = jnp.maximum(jnp.max(s_v, axis=1, keepdims=True), jnp.max(s_s, axis=1, keepdims=True))
        w_v = jnp.exp(s_v - m)
        w_s = jnp.exp(s_s - m)
        totals.append(jnp.sum(w_v, axis=1, keepdims=True) + jnp.sum(w_s, axis=1, keepdims=True))
        probs.append(w_v.astype(jnp.bfloat16))
        outs.append(jnp.dot(w_s.astype(jnp.bfloat16), v_s, preferred_element_type=jnp.float32))
    o_v = jnp.dot(jnp.concatenate(probs, axis=0), v_vert, preferred_element_type=jnp.float32)
    o = (o_v + jnp.concatenate(outs, axis=0)) / jnp.concatenate(totals, axis=0)
    att[:, lanes] = o.astype(jnp.bfloat16)


def spread(values, copies, width):
    lane = lax.broadcasted_iota(jnp.int32, (values.shape[0], copies * width), 1) // width
    out = jnp.zeros(lane.shape, jnp.int32)
    for j in range(copies):
        out = jnp.where(lane == j, values[:, j : j + 1], out)
    return out


def layer_kernel(
    vertical, slash, vert_v, slash_v, q_ref, k_ref, v_ref, w_hbm, out_ref,
    pool, window, bv, bs, slots_v, slots, att, w, to_sib, from_sib, to_cross, from_cross,
    slot_sem, w_sem, sib_send, sib_recv, cross_send, cross_recv, g_send, g_recv,
):
    heads, nv = vertical.shape
    ns = slash.shape[1]
    chunks = w.shape[0]
    quarter = out_ref.shape[0] // BLK
    blocks = k_ref.shape[0]
    reach = window.shape[0] - blocks
    t = lax.axis_index("tp")
    chip, core = t // 2, t % 2
    sibling = 2 * chip + (1 - core)
    cross = 2 * (1 - chip) + core
    me = lax.axis_index("ctx")
    z, x, y = me // (NX * NY), (me // NY) % NX, me % NY
    count = NZ * NX * NY

    def ctx(zz, xx, yy):
        return {"ctx": (zz % NZ) * (NX * NY) + xx * NY + yy % NY}

    after, before = {"ctx": (me + 1) % count}, {"ctx": (me + count - 1) % count}
    barrier = pltpu.get_barrier_semaphore()
    partners = [{"tp": sibling}, {"tp": cross}, after, before, ctx(z, 1 - x, y)]
    partners += [ctx(z, x, y + d) for d in range(1, NY)] + [ctx(z + d, x, y) for d in range(1, NZ)]
    for other in partners:
        pl.semaphore_signal(barrier, inc=1, device_id=other, device_id_type=MESH)

    def weights(c):
        at = pl.ds(pl.multiple_of(c * WIDE, WIDE), WIDE)
        return pltpu.make_async_copy(w_hbm.at[:, at], w.at[c], w_sem.at[c])

    @pl.loop(0, chunks)
    def _(c):
        weights(c).start()

    window[reach:, :, :HS] = k_ref[...]
    window[reach:, :, HS:] = v_ref[...]
    low, high = blocks - 1, 0
    for h in range(heads):
        for j in range(nv):
            v = vertical[h, j]
            mine = v // blocks == me
            low = jnp.minimum(low, jnp.where(mine, v % blocks, blocks - 1))
            high = jnp.maximum(high, jnp.where(mine, v % blocks, 0))
    pool[z, x, y, 0, :, :HS] = k_ref[low]
    pool[z, x, y, 0, :, HS:] = v_ref[low]
    pool[z, x, y, 1, :, :HS] = k_ref[high]
    pool[z, x, y, 1, :, HS:] = v_ref[high]

    pl.semaphore_wait(barrier, len(partners))

    def push(n, ref, to):
        return pltpu.make_async_remote_copy(
            src_ref=ref, dst_ref=ref, send_sem=g_send.at[n], recv_sem=g_recv.at[n],
            device_id=to, device_id_type=MESH,
        )

    def got(n, ref):
        push(n, ref, after).wait_recv()

    sent = []

    def send(n, ref, to):
        copy = push(n, ref, to)
        copy.start()
        sent.append(copy)

    up, down = (z + 1) % NZ, (z + NZ - 1) % NZ
    right, left = (y + 1) % NY, (y + NY - 1) % NY
    send(0, pool.at[z, x, y], ctx(z, 1 - x, y))
    near = pltpu.make_async_remote_copy(
        src_ref=window.at[pl.ds(reach, blocks)], dst_ref=window.at[pl.ds(reach - blocks, blocks)],
        send_sem=g_send.at[15], recv_sem=g_recv.at[15], device_id=after, device_id_type=MESH,
    )
    near.start()

    vert = vert_v[...]
    second = jnp.zeros((heads, nv), jnp.int32)
    for h in range(heads):
        for j in range(nv):
            v = vertical[h, j]
            second = jnp.where((vert // blocks == v // blocks) & (vert > v), 1, second)
    slots_v[...] = second
    place = pltpu.make_async_copy(slots_v, slots, slot_sem)
    place.start()
    vert_wide = spread(vert, nv, BLK)
    slash_wide = spread(slash_v[...], ns, BLK)
    for i in range(blocks):
        block = me * blocks + i
        away = block - vert_wide
        kept = away > 0
        for j in range(ns):
            kept = kept & (away != slash_v[:, j : j + 1])
        bv[i] = jnp.where(kept, 0.0, NEG)
        bs[i] = jnp.where(slash_wide <= block, 0.0, NEG)

    got(0, pool.at[z, 1 - x, y])
    for d in range(1, NY):
        send(d, pool.at[z, :, y, 0], ctx(z, x, y + d))
    for d in range(1, NZ):
        send(3 + d, pool.at[z, :, y, 1], ctx(z + d, x, y))
    for d in range(1, NY):
        got(d, pool.at[z, :, (y + NY - d) % NY, 0])
    send(7, pool.at[z, :, :, 0], ctx(z + 1, x, y))
    send(8, pool.at[z, :, :, 0], ctx(z + NZ - 1, x, y))
    for d in range(1, NZ):
        got(3 + d, pool.at[(z + NZ - d) % NZ, :, y, 1])
    send(9, pool.at[:, :, y, 1], ctx(z, x, y + 1))
    send(10, pool.at[:, :, y, 1], ctx(z, x, y + NY - 1))
    near.wait_recv()
    far = pltpu.make_async_remote_copy(
        src_ref=window.at[pl.ds(reach - blocks + 1, blocks - 1)],
        dst_ref=window.at[pl.ds(reach - 2 * blocks + 1, blocks - 1)],
        send_sem=g_send.at[16], recv_sem=g_recv.at[16], device_id=after, device_id_type=MESH,
    )
    far.start()
    got(7, pool.at[down, :, :, 0])
    send(11, pool.at[down, 0, :, 0], ctx(z + 1, x, y))
    got(8, pool.at[up, :, :, 0])
    send(12, pool.at[up, 1, :, 0], ctx(z + NZ - 1, x, y))
    got(9, pool.at[:, :, left, 1])
    send(13, pool.at[:, 0, left, 1], ctx(z, x, y + 1))
    got(10, pool.at[:, :, right, 1])
    send(14, pool.at[:, 1, right, 1], ctx(z, x, y + NY - 1))
    got(11, pool.at[(z + 2) % NZ, 0, :, 0])
    got(12, pool.at[(z + 2) % NZ, 1, :, 0])
    got(13, pool.at[:, 0, (y + 2) % NY, 1])
    got(14, pool.at[:, 1, (y + 2) % NY, 1])
    far.wait_recv()
    place.wait()

    def hand(k, c):
        return pltpu.make_async_remote_copy(
            src_ref=to_sib.at[k, c],
            dst_ref=from_sib.at[k, c],
            send_sem=sib_send.at[k, c],
            recv_sem=sib_recv.at[k, c],
            device_id={"tp": sibling},
            device_id_type=MESH,
        )

    def over(c):
        return pltpu.make_async_remote_copy(
            src_ref=to_cross.at[c],
            dst_ref=from_cross.at[c],
            send_sem=cross_send.at[c],
            recv_sem=cross_recv.at[c],
            device_id={"tp": cross},
            device_id_type=MESH,
        )

    @pl.loop(0, 4)
    def _(stage):
        there, swap = 1 - stage // 2, 1 - stage % 2
        owner = 2 * (chip + (1 - 2 * chip) * there) + core + (1 - 2 * core) * swap

        @pl.loop(0, heads)
        def _(h):
            attend_head(
                h, owner * quarter, slots, vertical, slash, q_ref, pool, window, bv, bs, att
            )

        @pl.loop(0, chunks)
        def _(c):
            @pl.when(stage == 0)
            def _():
                weights(c).wait()

            part = jnp.dot(att[...], w[c], preferred_element_type=jnp.float32)

            @pl.when(stage == 0)
            def _():
                to_sib[0, c] = part.astype(jnp.bfloat16)
                hand(0, c).start()

            @pl.when(stage == 1)
            def _():
                hand(0, c).wait_recv()
                to_cross[c] = (part + from_sib[0, c].astype(jnp.float32)).astype(jnp.bfloat16)
                over(c).start()

            @pl.when(stage == 2)
            def _():
                to_sib[1, c] = part.astype(jnp.bfloat16)
                hand(1, c).start()

            @pl.when(stage == 3)
            def _():
                hand(1, c).wait_recv()
                over(c).wait_recv()
                at = pl.ds(pl.multiple_of(c * WIDE, WIDE), WIDE)
                out_ref[:, at] = (
                    part + from_sib[1, c].astype(jnp.float32) + from_cross[c].astype(jnp.float32)
                ).astype(jnp.bfloat16)

    @pl.loop(0, chunks)
    def _(c):
        hand(0, c).wait_send()
        hand(1, c).wait_send()
        over(c).wait_send()

    for copy in sent + [near, far]:
        copy.wait_send()


def shards(queries, keys, values, out_weight, vertical, slash):
    rows, width = queries.shape
    heads, nv = vertical.shape
    ns = slash.shape[1]
    blocks = rows // BLK
    chunks = out_weight.shape[1] // WIDE
    part = (rows // 4, WIDE)
    vmem = pl.BlockSpec(memory_space=pltpu.VMEM)
    smem = pl.BlockSpec(memory_space=pltpu.SMEM)
    dma = pltpu.SemaphoreType.DMA
    return pl.pallas_call(
        layer_kernel,
        out_shape=jax.ShapeDtypeStruct((rows // 4, out_weight.shape[1]), jnp.bfloat16),
        in_specs=[smem, smem] + [vmem] * 5 + [pl.BlockSpec(memory_space=pl.ANY)],
        out_specs=vmem,
        scratch_shapes=[
            pltpu.VMEM((NZ, NX, NY, 2, BLK, 2 * HS), jnp.bfloat16),
            pltpu.VMEM((3 * blocks, BLK, 2 * HS), jnp.bfloat16),
            pltpu.VMEM((blocks, heads, nv * BLK), jnp.float32),
            pltpu.VMEM((blocks, heads, ns * BLK), jnp.float32),
            pltpu.VMEM((heads, nv), jnp.int32),
            pltpu.SMEM((heads, nv), jnp.int32),
            pltpu.VMEM((rows // 4, width), jnp.bfloat16),
            pltpu.VMEM((chunks, width, WIDE), jnp.bfloat16),
            pltpu.VMEM((2, chunks) + part, jnp.bfloat16),
            pltpu.VMEM((2, chunks) + part, jnp.bfloat16),
            pltpu.VMEM((chunks,) + part, jnp.bfloat16),
            pltpu.VMEM((chunks,) + part, jnp.bfloat16),
            dma,
            dma((chunks,)),
            dma((2, chunks)),
            dma((2, chunks)),
            dma((chunks,)),
            dma((chunks,)),
            dma((17,)),
            dma((17,)),
        ],
        compiler_params=pltpu.CompilerParams(
            collective_id=0, has_side_effects=True, vmem_limit_bytes=52 << 20
        ),
    )(
        vertical, slash, vertical, slash, queries, keys.reshape(blocks, BLK, HS),
        values.reshape(blocks, BLK, HS), out_weight,
    )


def solution(mesh):
    return jax.shard_map(
        shards,
        mesh=mesh,
        in_specs=(
            P("ctx", "tp"),
            P("ctx", "tp"),
            P("ctx", "tp"),
            P("tp", None),
            P("tp", None),
            P("tp", None),
        ),
        out_specs=P(("ctx", "tp"), None),
        check_vma=False,
    )
```

```python
import jax
import jax.numpy as jnp
from jax import lax
from jax.experimental import pallas as pl
from jax.experimental.pallas import tpu as pltpu
from jax.sharding import PartitionSpec as P

HS = 128
BLK = 64
NEG = -1e30
MESH = pl.DeviceIdType.MESH
WIDE = 1024
NZ, NX, NY = 4, 2, 4
PAIR = 2


def attend_head(h, places, slots, vertical, slash, queries, pool, window, bv, bs, out):
    nv, ns = vertical.shape[1], slash.shape[1]
    reach = window.shape[0] - queries.shape[0]
    scale = 1.0 / (HS**0.5)
    lanes = pl.ds(pl.multiple_of(h * HS, HS), HS)
    at_v = []
    for j in range(nv):
        s = vertical[h, j] // 8
        at_v.append((s // (NX * NY), (s // NY) % NX, s % NY, slots[h, j]))
    k_vert = jnp.concatenate([pool[a, b, c, d, :, :HS] for a, b, c, d in at_v], axis=0)
    v_vert = jnp.concatenate([pool[a, b, c, d, :, HS:] for a, b, c, d in at_v], axis=0)
    row = lax.broadcasted_iota(jnp.int32, (BLK, BLK), 0)
    col = lax.broadcasted_iota(jnp.int32, (BLK, BLK), 1)
    triangle = jnp.where(col > row, NEG, 0.0).astype(jnp.float32)
    triangle = jnp.concatenate([triangle, jnp.zeros((BLK, (ns - 1) * BLK), jnp.float32)], axis=1)
    q = jnp.concatenate([queries[i, :, lanes] for i in places], axis=0)
    s_vert = lax.dot_general(
        q, k_vert, (((1,), (1,)), ((), ())), preferred_element_type=jnp.float32
    )
    probs, outs, totals = [], [], []
    for half, i in enumerate(places):
        at = [reach + i - slash[h, j] for j in range(ns)]
        k_s = jnp.concatenate([window[a, :, :HS] for a in at], axis=0)
        v_s = jnp.concatenate([window[a, :, HS:] for a in at], axis=0)
        qi = q[half * BLK : (half + 1) * BLK]
        s_s = lax.dot_general(
            qi, k_s, (((1,), (1,)), ((), ())), preferred_element_type=jnp.float32
        )
        s_s = s_s * scale + (bs[i, pl.ds(h, 1), :] + triangle)
        s_v = s_vert[half * BLK : (half + 1) * BLK] * scale + bv[i, pl.ds(h, 1), :]
        m = jnp.maximum(jnp.max(s_v, axis=1, keepdims=True), jnp.max(s_s, axis=1, keepdims=True))
        w_v = jnp.exp(s_v - m)
        w_s = jnp.exp(s_s - m)
        totals.append(jnp.sum(w_v, axis=1, keepdims=True) + jnp.sum(w_s, axis=1, keepdims=True))
        probs.append(w_v.astype(jnp.bfloat16))
        outs.append(jnp.dot(w_s.astype(jnp.bfloat16), v_s, preferred_element_type=jnp.float32))
    o_v = jnp.dot(jnp.concatenate(probs, axis=0), v_vert, preferred_element_type=jnp.float32)
    o = (o_v + jnp.concatenate(outs, axis=0)) / jnp.concatenate(totals, axis=0)
    o = o.astype(jnp.bfloat16)
    out[0, :, lanes] = o[:BLK]
    out[1, :, lanes] = o[BLK:]


def spread(values, copies, width):
    lane = lax.broadcasted_iota(jnp.int32, (values.shape[0], copies * width), 1) // width
    out = jnp.zeros(lane.shape, jnp.int32)
    for j in range(copies):
        out = jnp.where(lane == j, values[:, j : j + 1], out)
    return out


def layer_kernel(
    vertical, slash, vert_hbm, slash_hbm, q_hbm, k_hbm, v_hbm, w_hbm, out_ref,
    k_ref, v_ref, vert_v, slash_v, queries, pool, window, bv, bs, slots_v, slots, att, w,
    to_sib, from_sib, to_cross, from_cross,
    in_sem, slot_sem, w_sem, sib_send, sib_recv, cross_send, cross_recv,
    lend_send, lend_recv, g_send, g_recv,
):
    heads, nv = vertical.shape
    ns = slash.shape[1]
    chunks = w.shape[0]
    blocks = k_hbm.shape[0]
    reach = window.shape[0] - blocks
    t = lax.axis_index("tp")
    chip, core = t // 2, t % 2
    sibling = 2 * chip + (1 - core)
    cross = 2 * (1 - chip) + core
    corner = 2 * (1 - chip) + (1 - core)
    me = lax.axis_index("ctx")
    z, x, y = me // (NX * NY), (me // NY) % NX, me % NY
    count = NZ * NX * NY

    def ctx(zz, xx, yy):
        return {"ctx": (zz % NZ) * (NX * NY) + xx * NY + yy % NY}

    after, before = {"ctx": (me + 1) % count}, {"ctx": (me + count - 1) % count}
    barrier = pltpu.get_barrier_semaphore()
    mirror = ctx(z, 1 - x, y)
    partners = [{"tp": sibling}, {"tp": cross}, {**mirror, "tp": cross}, after, before, mirror]
    partners += [ctx(z, x, y + d) for d in range(1, NY)] + [ctx(z + d, x, y) for d in range(1, NZ)]
    for other in partners:
        pl.semaphore_signal(barrier, inc=1, device_id=other, device_id_type=MESH)

    def weights(c):
        at = pl.ds(pl.multiple_of(c * WIDE, WIDE), WIDE)
        return pltpu.make_async_copy(w_hbm.at[:, at], w.at[c], w_sem.at[c])

    inputs = [
        (k_hbm, k_ref),
        (v_hbm, v_ref),
        (vert_hbm, vert_v),
        (slash_hbm, slash_v),
        (q_hbm, queries),
    ]
    inputs = [pltpu.make_async_copy(a, b, in_sem.at[n]) for n, (a, b) in enumerate(inputs)]
    for copy in inputs:
        copy.start()

    @pl.loop(0, chunks)
    def _(c):
        weights(c).start()

    low, high = blocks - 1, 0
    for h in range(heads):
        for j in range(nv):
            v = vertical[h, j]
            mine = v // blocks == me
            low = jnp.minimum(low, jnp.where(mine, v % blocks, blocks - 1))
            high = jnp.maximum(high, jnp.where(mine, v % blocks, 0))
    inputs[0].wait()
    inputs[1].wait()
    for half, kv in enumerate((k_ref, v_ref)):
        at = slice(half * HS, (half + 1) * HS)
        window[reach:, :, at] = kv[...]
        pool[z, x, y, 0, :, at] = kv[low]
        pool[z, x, y, 1, :, at] = kv[high]

    pl.semaphore_wait(barrier, len(partners))

    def push(n, ref, to):
        return pltpu.make_async_remote_copy(
            src_ref=ref, dst_ref=ref, send_sem=g_send.at[n], recv_sem=g_recv.at[n],
            device_id=to, device_id_type=MESH,
        )

    def got(n, ref):
        push(n, ref, after).wait_recv()

    sent = []

    def send(n, ref, to):
        copy = push(n, ref, to)
        copy.start()
        sent.append(copy)

    up, down = (z + 1) % NZ, (z + NZ - 1) % NZ
    right, left = (y + 1) % NY, (y + NY - 1) % NY
    send(0, pool.at[z, x, y], mirror)
    near = pltpu.make_async_remote_copy(
        src_ref=window.at[pl.ds(reach, blocks)], dst_ref=window.at[pl.ds(reach - blocks, blocks)],
        send_sem=g_send.at[15], recv_sem=g_recv.at[15], device_id=after, device_id_type=MESH,
    )
    near.start()

    for copy in inputs[2:]:
        copy.wait()
    vert = vert_v[...]
    second = jnp.zeros((heads, nv), jnp.int32)
    for h in range(heads):
        for j in range(nv):
            v = vertical[h, j]
            second = jnp.where((vert // blocks == v // blocks) & (vert > v), 1, second)
    slots_v[...] = second
    place = pltpu.make_async_copy(slots_v, slots, slot_sem)
    place.start()
    vert_wide = spread(vert, nv, BLK)
    slash_wide = spread(slash_v[...], ns, BLK)
    for i in range(blocks):
        block = me * blocks + i
        away = block - vert_wide
        kept = away > 0
        for j in range(ns):
            kept = kept & (away != slash_v[:, j : j + 1])
        bv[i] = jnp.where(kept, 0.0, NEG)
        bs[i] = jnp.where(slash_wide <= block, 0.0, NEG)

    got(0, pool.at[z, 1 - x, y])
    for d in range(1, NY):
        send(d, pool.at[z, :, y, 0], ctx(z, x, y + d))
    for d in range(1, NZ):
        send(3 + d, pool.at[z, :, y, 1], ctx(z + d, x, y))
    for d in range(1, NY):
        got(d, pool.at[z, :, (y + NY - d) % NY, 0])
    send(7, pool.at[z, :, :, 0], ctx(z + 1, x, y))
    send(8, pool.at[z, :, :, 0], ctx(z + NZ - 1, x, y))
    for d in range(1, NZ):
        got(3 + d, pool.at[(z + NZ - d) % NZ, :, y, 1])
    send(9, pool.at[:, :, y, 1], ctx(z, x, y + 1))
    send(10, pool.at[:, :, y, 1], ctx(z, x, y + NY - 1))
    near.wait_recv()
    far = pltpu.make_async_remote_copy(
        src_ref=window.at[pl.ds(reach - blocks + 1, blocks - 1)],
        dst_ref=window.at[pl.ds(reach - 2 * blocks + 1, blocks - 1)],
        send_sem=g_send.at[16], recv_sem=g_recv.at[16], device_id=after, device_id_type=MESH,
    )
    far.start()
    got(7, pool.at[down, :, :, 0])
    send(11, pool.at[down, 0, :, 0], ctx(z + 1, x, y))
    got(8, pool.at[up, :, :, 0])
    send(12, pool.at[up, 1, :, 0], ctx(z + NZ - 1, x, y))
    got(9, pool.at[:, :, left, 1])
    send(13, pool.at[:, 0, left, 1], ctx(z, x, y + 1))
    got(10, pool.at[:, :, right, 1])
    send(14, pool.at[:, 1, right, 1], ctx(z, x, y + NY - 1))
    got(11, pool.at[(z + 2) % NZ, 0, :, 0])
    got(12, pool.at[(z + 2) % NZ, 1, :, 0])
    got(13, pool.at[:, 0, (y + 2) % NY, 1])
    got(14, pool.at[:, 1, (y + 2) % NY, 1])
    far.wait_recv()
    place.wait()

    def hand(k, c):
        return pltpu.make_async_remote_copy(
            src_ref=to_sib.at[k, c],
            dst_ref=from_sib.at[k, c],
            send_sem=sib_send.at[k, c],
            recv_sem=sib_recv.at[k, c],
            device_id={"tp": sibling},
            device_id_type=MESH,
        )

    def over(half, c):
        to = {"tp": cross} if half == 0 else {**mirror, "tp": cross}
        return pltpu.make_async_remote_copy(
            src_ref=to_cross.at[c, half],
            dst_ref=from_cross.at[c, half],
            send_sem=cross_send.at[half, c],
            recv_sem=cross_recv.at[half, c],
            device_id=to,
            device_id_type=MESH,
        )

    def lend(n):
        at = pl.ds(pl.multiple_of(n * PAIR * HS, PAIR * HS), PAIR * HS)
        return pltpu.make_async_remote_copy(
            src_ref=att.at[0, :, :, at],
            dst_ref=att.at[2, :, :, at],
            send_sem=lend_send.at[n],
            recv_sem=lend_recv.at[n],
            device_id=mirror,
            device_id_type=MESH,
        )

    def attend(h, places, out):
        attend_head(h, places, slots, vertical, slash, queries, pool, window, bv, bs, att.at[out])

    def project(first, second, c):
        rows = jnp.concatenate([att[first], att[second]], axis=0)
        return jnp.dot(rows, w[c], preferred_element_type=jnp.float32)

    @pl.loop(0, heads)
    def _(h):
        attend(h, (2 * corner + 1, 2 * cross + 1), 0)

        @pl.when(h % PAIR == PAIR - 1)
        def _():
            lend(h // PAIR).start()

    @pl.loop(0, heads)
    def _(h):
        attend(h, (2 * corner, 2 * cross), 1)

    for n in range(heads // PAIR):
        lend(n).wait_recv()

    @pl.loop(0, chunks)
    def _(c):
        weights(c).wait()
        to_sib[0, c] = project((1, 0), (2, 0), c).astype(jnp.bfloat16)
        hand(0, c).start()

    @pl.loop(0, chunks)
    def _(c):
        part = project((1, 1), (2, 1), c)
        hand(0, c).wait_recv()
        part = (part + from_sib[0, c].astype(jnp.float32)).astype(jnp.bfloat16)
        to_cross[c, 0] = part[:BLK]
        to_cross[c, 1] = part[BLK:]
        over(0, c).start()
        over(1, c).start()

    @pl.loop(0, heads)
    def _(h):
        attend(h, (2 * sibling, 2 * sibling + 1), 3)

    @pl.loop(0, chunks)
    def _(c):
        to_sib[1, c] = project((3, 0), (3, 1), c).astype(jnp.bfloat16)
        hand(1, c).start()

    @pl.loop(0, heads)
    def _(h):
        attend(h, (2 * t, 2 * t + 1), 4)

    @pl.loop(0, chunks)
    def _(c):
        part = project((4, 0), (4, 1), c)
        hand(1, c).wait_recv()
        part = part + from_sib[1, c].astype(jnp.float32)
        at = pl.ds(pl.multiple_of(c * WIDE, WIDE), WIDE)
        for half in range(2):
            over(half, c).wait_recv()
            here = part[half * BLK : (half + 1) * BLK]
            out_ref[half * BLK : (half + 1) * BLK, at] = (
                here + from_cross[c, half].astype(jnp.float32)
            ).astype(jnp.bfloat16)

    @pl.loop(0, chunks)
    def _(c):
        hand(0, c).wait_send()
        hand(1, c).wait_send()
        over(0, c).wait_send()
        over(1, c).wait_send()

    for n in range(heads // PAIR):
        lend(n).wait_send()

    for copy in sent + [near, far]:
        copy.wait_send()


def shards(queries, keys, values, out_weight, vertical, slash):
    rows, width = queries.shape
    heads, nv = vertical.shape
    ns = slash.shape[1]
    blocks = rows // BLK
    chunks = out_weight.shape[1] // WIDE
    part = (rows // 4, WIDE)
    vmem = pl.BlockSpec(memory_space=pltpu.VMEM)
    smem = pl.BlockSpec(memory_space=pltpu.SMEM)
    dma = pltpu.SemaphoreType.DMA
    return pl.pallas_call(
        layer_kernel,
        out_shape=jax.ShapeDtypeStruct((rows // 4, out_weight.shape[1]), jnp.bfloat16),
        in_specs=[smem, smem] + [pl.BlockSpec(memory_space=pltpu.HBM)] * 6,
        out_specs=vmem,
        scratch_shapes=[
            pltpu.VMEM((blocks, BLK, HS), jnp.bfloat16),
            pltpu.VMEM((blocks, BLK, HS), jnp.bfloat16),
            pltpu.VMEM((heads, nv), jnp.int32),
            pltpu.VMEM((heads, ns), jnp.int32),
            pltpu.VMEM((blocks, BLK, width), jnp.bfloat16),
            pltpu.VMEM((NZ, NX, NY, 2, BLK, 2 * HS), jnp.bfloat16),
            pltpu.VMEM((3 * blocks, BLK, 2 * HS), jnp.bfloat16),
            pltpu.VMEM((blocks, heads, nv * BLK), jnp.float32),
            pltpu.VMEM((blocks, heads, ns * BLK), jnp.float32),
            pltpu.VMEM((heads, nv), jnp.int32),
            pltpu.SMEM((heads, nv), jnp.int32),
            pltpu.VMEM((5, 2, BLK, width), jnp.bfloat16),
            pltpu.VMEM((chunks, width, WIDE), jnp.bfloat16),
            pltpu.VMEM((2, chunks) + part, jnp.bfloat16),
            pltpu.VMEM((2, chunks) + part, jnp.bfloat16),
            pltpu.VMEM((chunks, 2, BLK, WIDE), jnp.bfloat16),
            pltpu.VMEM((chunks, 2, BLK, WIDE), jnp.bfloat16),
            dma((5,)),
            dma,
            dma((chunks,)),
            dma((2, chunks)),
            dma((2, chunks)),
            dma((2, chunks)),
            dma((2, chunks)),
            dma((heads // PAIR,)),
            dma((heads // PAIR,)),
            dma((17,)),
            dma((17,)),
        ],
        compiler_params=pltpu.CompilerParams(
            collective_id=0, has_side_effects=True, vmem_limit_bytes=60 << 20
        ),
    )(
        vertical, slash, vertical, slash, queries.reshape(blocks, BLK, width),
        keys.reshape(blocks, BLK, HS),
        values.reshape(blocks, BLK, HS), out_weight,
    )


def solution(mesh):
    return jax.shard_map(
        shards,
        mesh=mesh,
        in_specs=(
            P("ctx", "tp"),
            P("ctx", "tp"),
            P("ctx", "tp"),
            P("tp", None),
            P("tp", None),
            P("tp", None),
        ),
        out_specs=P(("ctx", "tp"), None),
        check_vma=False,
    )
```

```python
import jax
import jax.numpy as jnp
from jax import lax
from jax.experimental import pallas as pl
from jax.experimental.pallas import tpu as pltpu
from jax.sharding import PartitionSpec as P

HS = 128
BLK = 64
NEG = -1e30
MESH = pl.DeviceIdType.MESH
WIDE = 1024
NZ, NX, NY = 4, 2, 4
TOGETHER = 2


def attend_heads(hs, places, slots, slash, queries, pool, window, bv, bs, att, to):
    nv, ns = slots.shape[1], slash.shape[1]
    reach = window.shape[0] - queries.shape[0]
    scale = 1.4426950408889634 / (HS**0.5)
    over_keys = (((1,), (1,)), ((), ()))
    row = lax.broadcasted_iota(jnp.int32, (BLK, BLK), 0)
    col = lax.broadcasted_iota(jnp.int32, (BLK, BLK), 1)
    triangle = jnp.where(col > row, NEG, 0.0).astype(jnp.float32)
    lanes = [pl.ds(pl.multiple_of(h * HS, HS), HS) for h in hs]
    scores, v_vert, v_slash = [], [], []
    for h, lane in zip(hs, lanes):
        at_v = [slots[h, j] for j in range(nv)]
        k_vert = jnp.concatenate([pool[a, :, :HS] for a in at_v], axis=0)
        v_vert.append(jnp.concatenate([pool[a, :, HS:] for a in at_v], axis=0))
        q = jnp.concatenate([queries[i, :, lane] for i in places], axis=0)
        s_vert = lax.dot_general(q, k_vert, over_keys, preferred_element_type=jnp.float32)
        for n, i in enumerate(places):
            at = [reach + i - slash[h, j] for j in range(ns)]
            k_s = jnp.concatenate([window[a, :, :HS] for a in at], axis=0)
            v_slash.append(jnp.concatenate([window[a, :, HS:] for a in at], axis=0))
            rows = slice(n * BLK, (n + 1) * BLK)
            s_s = lax.dot_general(q[rows], k_s, over_keys, preferred_element_type=jnp.float32)
            scores.append((s_vert[rows], s_s, bv[i, pl.ds(h, 1), :], bs[i, pl.ds(h, 1), :]))
    weights, totals = [], []
    for s_v, s_s, b_v, b_s in scores:
        s_v = s_v + b_v
        s_s = jnp.concatenate([s_s[:, :BLK] + triangle, s_s[:, BLK:]], axis=1) + b_s
        m = jnp.maximum(jnp.max(s_v, axis=1, keepdims=True), jnp.max(s_s, axis=1, keepdims=True))
        w_v, w_s = jnp.exp2((s_v - m) * scale), jnp.exp2((s_s - m) * scale)
        totals.append(jnp.sum(w_v, axis=1, keepdims=True) + jnp.sum(w_s, axis=1, keepdims=True))
        weights.append((w_v.astype(jnp.bfloat16), w_s.astype(jnp.bfloat16)))
    for n, lane in enumerate(lanes):
        own = range(n * len(places), (n + 1) * len(places))
        o_v = jnp.dot(
            jnp.concatenate([weights[k][0] for k in own], axis=0), v_vert[n],
            preferred_element_type=jnp.float32,
        )
        for k, (slot, half) in zip(own, to):
            o_s = jnp.dot(weights[k][1], v_slash[k], preferred_element_type=jnp.float32)
            at = k - own[0]
            o = (o_v[at * BLK : (at + 1) * BLK] + o_s) / totals[k]
            att[slot, half, :, lane] = o.astype(jnp.bfloat16)


def spread(values, copies, width):
    lane = lax.broadcasted_iota(jnp.int32, (values.shape[0], copies * width), 1) // width
    out = jnp.zeros(lane.shape, jnp.int32)
    for j in range(copies):
        out = jnp.where(lane == j, values[:, j : j + 1], out)
    return out


def layer_kernel(
    vertical, slash, vert_hbm, slash_hbm, q_hbm, k_hbm, v_hbm, w_hbm, out_ref,
    k_ref, v_ref, vert_v, slash_v, queries, pool, window, bv, bs, slots_v, slots, att, w,
    to_sib, from_sib, to_cross, from_cross, kept_back, held,
    in_sem, slot_sem, w_sem, sib_send, sib_recv, cross_send, cross_recv,
    lend_send, lend_recv, g_send, g_recv,
):
    heads, nv = vertical.shape
    ns = slash.shape[1]
    chunks = w.shape[0]
    blocks = k_hbm.shape[0]
    reach = window.shape[0] - blocks
    t = lax.axis_index("tp")
    chip, core = t // 2, t % 2
    sibling = 2 * chip + (1 - core)
    cross = 2 * (1 - chip) + core
    corner = 2 * (1 - chip) + (1 - core)
    me = lax.axis_index("ctx")
    z, x, y = me // (NX * NY), (me // NY) % NX, me % NY
    count = NZ * NX * NY

    def ctx(zz, xx, yy):
        return {"ctx": (zz % NZ) * (NX * NY) + xx * NY + yy % NY}

    after, before = {"ctx": (me + 1) % count}, {"ctx": (me + count - 1) % count}
    barrier = pltpu.get_barrier_semaphore()
    mirror = ctx(z, 1 - x, y)
    partners = [{"tp": sibling}, {"tp": cross}, {**mirror, "tp": cross}, after, before, mirror]
    partners += [ctx(z, x, y + d) for d in range(1, NY)] + [ctx(z + d, x, y) for d in range(1, NZ)]
    for other in partners:
        pl.semaphore_signal(barrier, inc=1, device_id=other, device_id_type=MESH)

    def weights(c):
        at = pl.ds(pl.multiple_of(c * WIDE, WIDE), WIDE)
        return pltpu.make_async_copy(w_hbm.at[:, at], w.at[c], w_sem.at[c])

    inputs = [
        (k_hbm, k_ref),
        (v_hbm, v_ref),
        (vert_hbm, vert_v),
        (slash_hbm, slash_v),
        (q_hbm, queries),
    ]
    inputs = [pltpu.make_async_copy(a, b, in_sem.at[n]) for n, (a, b) in enumerate(inputs)]
    for copy in inputs:
        copy.start()

    @pl.loop(0, chunks)
    def _(c):
        weights(c).start()

    low, high = blocks - 1, 0
    for h in range(heads):
        for j in range(nv):
            v = vertical[h, j]
            mine = v // blocks == me
            low = jnp.minimum(low, jnp.where(mine, v % blocks, blocks - 1))
            high = jnp.maximum(high, jnp.where(mine, v % blocks, 0))
    inputs[0].wait()
    inputs[1].wait()
    for half, kv in enumerate((k_ref, v_ref)):
        at = slice(half * HS, (half + 1) * HS)
        window[reach:, :, at] = kv[...]
        pool[z, x, y, 0, :, at] = kv[low]
        pool[z, x, y, 1, :, at] = kv[high]

    pl.semaphore_wait(barrier, len(partners))

    def push(n, ref, to):
        return pltpu.make_async_remote_copy(
            src_ref=ref, dst_ref=ref, send_sem=g_send.at[n], recv_sem=g_recv.at[n],
            device_id=to, device_id_type=MESH,
        )

    def got(n, ref):
        push(n, ref, after).wait_recv()

    sent = []

    def send(n, ref, to):
        copy = push(n, ref, to)
        copy.start()
        sent.append(copy)

    up, down = (z + 1) % NZ, (z + NZ - 1) % NZ
    right, left = (y + 1) % NY, (y + NY - 1) % NY
    send(0, pool.at[z, x, y], mirror)
    near = pltpu.make_async_remote_copy(
        src_ref=window.at[pl.ds(reach, blocks)], dst_ref=window.at[pl.ds(reach - blocks, blocks)],
        send_sem=g_send.at[15], recv_sem=g_recv.at[15], device_id=after, device_id_type=MESH,
    )
    near.start()

    for copy in inputs[2:]:
        copy.wait()
    vert = vert_v[...]
    second = jnp.zeros((heads, nv), jnp.int32)
    for h in range(heads):
        for j in range(nv):
            v = vertical[h, j]
            second = jnp.where((vert // blocks == v // blocks) & (vert > v), 1, second)
    slots_v[...] = 2 * (vert // blocks) + second
    place = pltpu.make_async_copy(slots_v, slots, slot_sem)
    place.start()
    vert_wide = spread(vert, nv, BLK)
    slash_wide = spread(slash_v[...], ns, BLK)
    for i in range(blocks):
        block = me * blocks + i
        away = block - vert_wide
        kept = away > 0
        for j in range(ns):
            kept = kept & (away != slash_v[:, j : j + 1])
        bv[i] = jnp.where(kept, 0.0, NEG)
        bs[i] = jnp.where(slash_wide <= block, 0.0, NEG)

    got(0, pool.at[z, 1 - x, y])
    for d in range(1, NY):
        send(d, pool.at[z, :, y, 0], ctx(z, x, y + d))
    for d in range(1, NZ):
        send(3 + d, pool.at[z, :, y, 1], ctx(z + d, x, y))
    for d in range(1, NY):
        got(d, pool.at[z, :, (y + NY - d) % NY, 0])
    send(7, pool.at[z, :, :, 0], ctx(z + 1, x, y))
    send(8, pool.at[z, :, :, 0], ctx(z + NZ - 1, x, y))
    for d in range(1, NZ):
        got(3 + d, pool.at[(z + NZ - d) % NZ, :, y, 1])
    send(9, pool.at[:, :, y, 1], ctx(z, x, y + 1))
    send(10, pool.at[:, :, y, 1], ctx(z, x, y + NY - 1))
    near.wait_recv()
    far = pltpu.make_async_remote_copy(
        src_ref=window.at[pl.ds(reach - blocks + 1, blocks - 1)],
        dst_ref=window.at[pl.ds(reach - 2 * blocks + 1, blocks - 1)],
        send_sem=g_send.at[16], recv_sem=g_recv.at[16], device_id=after, device_id_type=MESH,
    )
    far.start()
    got(7, pool.at[down, :, :, 0])
    send(11, pool.at[down, 0, :, 0], ctx(z + 1, x, y))
    got(8, pool.at[up, :, :, 0])
    send(12, pool.at[up, 1, :, 0], ctx(z + NZ - 1, x, y))
    got(9, pool.at[:, :, left, 1])
    send(13, pool.at[:, 0, left, 1], ctx(z, x, y + 1))
    got(10, pool.at[:, :, right, 1])
    send(14, pool.at[:, 1, right, 1], ctx(z, x, y + NY - 1))
    got(11, pool.at[(z + 2) % NZ, 0, :, 0])
    got(12, pool.at[(z + 2) % NZ, 1, :, 0])
    got(13, pool.at[:, 0, (y + 2) % NY, 1])
    got(14, pool.at[:, 1, (y + 2) % NY, 1])
    far.wait_recv()
    place.wait()

    def hand(k, c):
        return pltpu.make_async_remote_copy(
            src_ref=to_sib.at[k, c],
            dst_ref=from_sib.at[k, c],
            send_sem=sib_send.at[k, c],
            recv_sem=sib_recv.at[k, c],
            device_id={"tp": sibling},
            device_id_type=MESH,
        )

    def over(half, c):
        to = {"tp": cross} if half == 0 else {**mirror, "tp": cross}
        return pltpu.make_async_remote_copy(
            src_ref=to_cross.at[c, half],
            dst_ref=from_cross.at[c, half],
            send_sem=cross_send.at[half, c],
            recv_sem=cross_recv.at[half, c],
            device_id=to,
            device_id_type=MESH,
        )

    def lend(n):
        at = pl.ds(pl.multiple_of(n * TOGETHER * HS, TOGETHER * HS), TOGETHER * HS)
        return pltpu.make_async_remote_copy(
            src_ref=att.at[0, :, :, at],
            dst_ref=att.at[2, :, :, at],
            send_sem=lend_send.at[n],
            recv_sem=lend_recv.at[n],
            device_id=mirror,
            device_id_type=MESH,
        )

    blocks_of_pool = pool.reshape(count * 2, BLK, 2 * HS)

    def attend(n, places, to):
        hs = [TOGETHER * n + k for k in range(TOGETHER)]
        attend_heads(hs, places, slots, slash, queries, blocks_of_pool, window, bv, bs, att, to)

    def project(parts, c):
        rows = jnp.concatenate([att[a, b] for a, b in parts], axis=0)
        return jnp.dot(rows, w[c], preferred_element_type=jnp.float32)

    @pl.loop(0, heads // TOGETHER)
    def _(n):
        places = (2 * corner + 1, 2 * cross + 1, 2 * corner, 2 * cross)
        attend(n, places, ((0, 0), (0, 1), (1, 0), (1, 1)))
        lend(n).start()

    for n in range(heads // TOGETHER):
        lend(n).wait_recv()

    def pass_on(c):
        hand(0, c).wait_recv()
        part = kept_back[c % 2] + from_sib[0, c].astype(jnp.float32)
        for half in range(2):
            to_cross[c, half] = part[half * BLK : (half + 1) * BLK].astype(jnp.bfloat16)
            over(half, c).start()

    @pl.loop(0, chunks)
    def _(c):
        weights(c).wait()
        part = project(((1, 0), (2, 0), (1, 1), (2, 1)), c)
        to_sib[0, c] = part[: 2 * BLK].astype(jnp.bfloat16)
        hand(0, c).start()
        kept_back[c % 2] = part[2 * BLK :]

        @pl.when(c > 0)
        def _():
            pass_on(c - 1)

    pass_on(chunks - 1)

    @pl.loop(0, heads // TOGETHER)
    def _(n):
        places = (2 * sibling, 2 * sibling + 1, 2 * t, 2 * t + 1)
        attend(n, places, ((3, 0), (3, 1), (4, 0), (4, 1)))

    @pl.loop(0, chunks)
    def _(c):
        part = project(((3, 0), (3, 1), (4, 0), (4, 1)), c)
        to_sib[1, c] = part[: 2 * BLK].astype(jnp.bfloat16)
        hand(1, c).start()
        held[c] = part[2 * BLK :]

    @pl.loop(0, chunks)
    def _(c):
        hand(1, c).wait_recv()
        part = held[c] + from_sib[1, c].astype(jnp.float32)
        at = pl.ds(pl.multiple_of(c * WIDE, WIDE), WIDE)
        for half in range(2):
            over(half, c).wait_recv()
            here = part[half * BLK : (half + 1) * BLK]
            out_ref[half * BLK : (half + 1) * BLK, at] = (
                here + from_cross[c, half].astype(jnp.float32)
            ).astype(jnp.bfloat16)

    @pl.loop(0, chunks)
    def _(c):
        hand(0, c).wait_send()
        hand(1, c).wait_send()
        over(0, c).wait_send()
        over(1, c).wait_send()

    for n in range(heads // TOGETHER):
        lend(n).wait_send()

    for copy in sent + [near, far]:
        copy.wait_send()


def shards(queries, keys, values, out_weight, vertical, slash):
    rows, width = queries.shape
    heads, nv = vertical.shape
    ns = slash.shape[1]
    blocks = rows // BLK
    chunks = out_weight.shape[1] // WIDE
    part = (rows // 4, WIDE)
    vmem = pl.BlockSpec(memory_space=pltpu.VMEM)
    smem = pl.BlockSpec(memory_space=pltpu.SMEM)
    dma = pltpu.SemaphoreType.DMA
    return pl.pallas_call(
        layer_kernel,
        out_shape=jax.ShapeDtypeStruct((rows // 4, out_weight.shape[1]), jnp.bfloat16),
        in_specs=[smem, smem] + [pl.BlockSpec(memory_space=pltpu.HBM)] * 6,
        out_specs=vmem,
        scratch_shapes=[
            pltpu.VMEM((blocks, BLK, HS), jnp.bfloat16),
            pltpu.VMEM((blocks, BLK, HS), jnp.bfloat16),
            pltpu.VMEM((heads, nv), jnp.int32),
            pltpu.VMEM((heads, ns), jnp.int32),
            pltpu.VMEM((blocks, BLK, width), jnp.bfloat16),
            pltpu.VMEM((NZ, NX, NY, 2, BLK, 2 * HS), jnp.bfloat16),
            pltpu.VMEM((3 * blocks, BLK, 2 * HS), jnp.bfloat16),
            pltpu.VMEM((blocks, heads, nv * BLK), jnp.float32),
            pltpu.VMEM((blocks, heads, ns * BLK), jnp.float32),
            pltpu.VMEM((heads, nv), jnp.int32),
            pltpu.SMEM((heads, nv), jnp.int32),
            pltpu.VMEM((5, 2, BLK, width), jnp.bfloat16),
            pltpu.VMEM((chunks, width, WIDE), jnp.bfloat16),
            pltpu.VMEM((2, chunks) + part, jnp.bfloat16),
            pltpu.VMEM((2, chunks) + part, jnp.bfloat16),
            pltpu.VMEM((chunks, 2, BLK, WIDE), jnp.bfloat16),
            pltpu.VMEM((chunks, 2, BLK, WIDE), jnp.bfloat16),
            pltpu.VMEM((2,) + part, jnp.float32),
            pltpu.VMEM((chunks,) + part, jnp.float32),
            dma((5,)),
            dma,
            dma((chunks,)),
            dma((2, chunks)),
            dma((2, chunks)),
            dma((2, chunks)),
            dma((2, chunks)),
            dma((heads // TOGETHER,)),
            dma((heads // TOGETHER,)),
            dma((17,)),
            dma((17,)),
        ],
        compiler_params=pltpu.CompilerParams(
            collective_id=0, has_side_effects=True, vmem_limit_bytes=60 << 20
        ),
    )(
        vertical, slash, vertical, slash, queries.reshape(blocks, BLK, width),
        keys.reshape(blocks, BLK, HS),
        values.reshape(blocks, BLK, HS), out_weight,
    )


def solution(mesh):
    return jax.shard_map(
        shards,
        mesh=mesh,
        in_specs=(
            P("ctx", "tp"),
            P("ctx", "tp"),
            P("ctx", "tp"),
            P("tp", None),
            P("tp", None),
            P("tp", None),
        ),
        out_specs=P(("ctx", "tp"), None),
        check_vma=False,
    )
```

```python
import jax
import jax.numpy as jnp
from jax import lax
from jax.experimental import pallas as pl
from jax.experimental.pallas import tpu as pltpu
from jax.sharding import PartitionSpec as P

HS = 128
BLK = 64
NEG = -1e30
MESH = pl.DeviceIdType.MESH
WIDE = 1024
NZ, NX, NY = 4, 2, 4
TOGETHER = 2
BEHIND = 3
AHEAD = 1


def attend_heads(hs, places, slots, slash, queries, pool, window, bv, bs, att, to):
    nv, ns = slots.shape[1], slash.shape[1]
    reach = window.shape[0] - queries.shape[0]
    scale = 1.4426950408889634 / (HS**0.5)
    over_keys = (((1,), (1,)), ((), ()))
    row = lax.broadcasted_iota(jnp.int32, (BLK, BLK), 0)
    col = lax.broadcasted_iota(jnp.int32, (BLK, BLK), 1)
    triangle = jnp.where(col > row, NEG, 0.0).astype(jnp.float32)
    lanes = [pl.ds(pl.multiple_of(h * HS, HS), HS) for h in hs]
    scores, v_vert, v_slash = [], [], []
    for h, lane in zip(hs, lanes):
        at_v = [slots[h, j] for j in range(nv)]
        k_vert = jnp.concatenate([pool[a, :, :HS] for a in at_v], axis=0)
        v_vert.append(jnp.concatenate([pool[a, :, HS:] for a in at_v], axis=0))
        q = jnp.concatenate([queries[i, :, lane] for i in places], axis=0)
        s_vert = lax.dot_general(q, k_vert, over_keys, preferred_element_type=jnp.float32)
        for n, i in enumerate(places):
            at = [reach + i - slash[h, j] for j in range(ns)]
            k_s = jnp.concatenate([window[a, :, :HS] for a in at], axis=0)
            v_slash.append(jnp.concatenate([window[a, :, HS:] for a in at], axis=0))
            rows = slice(n * BLK, (n + 1) * BLK)
            s_s = lax.dot_general(q[rows], k_s, over_keys, preferred_element_type=jnp.float32)
            scores.append((s_vert[rows], s_s, bv[i, pl.ds(h, 1), :], bs[i, pl.ds(h, 1), :]))
    weights, totals = [], []
    for s_v, s_s, b_v, b_s in scores:
        s_v = s_v + b_v
        s_s = jnp.concatenate([s_s[:, :BLK] + triangle, s_s[:, BLK:]], axis=1) + b_s
        m = jnp.maximum(jnp.max(s_v, axis=1, keepdims=True), jnp.max(s_s, axis=1, keepdims=True))
        w_v, w_s = jnp.exp2((s_v - m) * scale), jnp.exp2((s_s - m) * scale)
        totals.append(jnp.sum(w_v, axis=1, keepdims=True) + jnp.sum(w_s, axis=1, keepdims=True))
        weights.append((w_v.astype(jnp.bfloat16), w_s.astype(jnp.bfloat16)))
    for n, lane in enumerate(lanes):
        own = range(n * len(places), (n + 1) * len(places))
        o_v = jnp.dot(
            jnp.concatenate([weights[k][0] for k in own], axis=0), v_vert[n],
            preferred_element_type=jnp.float32,
        )
        for k, (slot, half) in zip(own, to):
            o_s = jnp.dot(weights[k][1], v_slash[k], preferred_element_type=jnp.float32)
            at = k - own[0]
            o = (o_v[at * BLK : (at + 1) * BLK] + o_s) / totals[k]
            att[slot, half, :, lane] = o.astype(jnp.bfloat16)


def spread(values, copies, width):
    lane = lax.broadcasted_iota(jnp.int32, (values.shape[0], copies * width), 1) // width
    out = jnp.zeros(lane.shape, jnp.int32)
    for j in range(copies):
        out = jnp.where(lane == j, values[:, j : j + 1], out)
    return out


def layer_kernel(
    vertical, slash, vert_hbm, slash_hbm, q_hbm, k_hbm, v_hbm, w_hbm, out_ref,
    k_ref, v_ref, vert_v, slash_v, queries, pool, window, bv, bs, slots_v, slots, att, w,
    to_sib, from_sib, to_cross, from_cross, kept_back, held,
    in_sem, slot_sem, w_sem, sib_send, sib_recv, cross_send, cross_recv,
    lend_send, lend_recv, g_send, g_recv,
):
    heads, nv = vertical.shape
    ns = slash.shape[1]
    chunks = w.shape[0]
    blocks = k_hbm.shape[0]
    reach = window.shape[0] - blocks
    t = lax.axis_index("tp")
    chip, core = t // 2, t % 2
    sibling = 2 * chip + (1 - core)
    cross = 2 * (1 - chip) + core
    corner = 2 * (1 - chip) + (1 - core)
    me = lax.axis_index("ctx")
    z, x, y = me // (NX * NY), (me // NY) % NX, me % NY
    count = NZ * NX * NY

    def ctx(zz, xx, yy):
        return {"ctx": (zz % NZ) * (NX * NY) + xx * NY + yy % NY}

    after, before = {"ctx": (me + 1) % count}, {"ctx": (me + count - 1) % count}
    barrier = pltpu.get_barrier_semaphore()
    mirror = ctx(z, 1 - x, y)
    partners = [{"tp": sibling}, {"tp": cross}, {**mirror, "tp": cross}, after, before, mirror]
    partners += [ctx(z, x, y + d) for d in range(1, NY)] + [ctx(z + d, x, y) for d in range(1, NZ)]
    for other in partners:
        pl.semaphore_signal(barrier, inc=1, device_id=other, device_id_type=MESH)

    def weights(c):
        at = pl.ds(pl.multiple_of(c * WIDE, WIDE), WIDE)
        return pltpu.make_async_copy(w_hbm.at[:, at], w.at[c], w_sem.at[c])

    inputs = [
        (k_hbm, k_ref),
        (v_hbm, v_ref),
        (vert_hbm, vert_v),
        (slash_hbm, slash_v),
        (q_hbm, queries),
    ]
    inputs = [pltpu.make_async_copy(a, b, in_sem.at[n]) for n, (a, b) in enumerate(inputs)]
    for copy in inputs:
        copy.start()

    @pl.loop(0, chunks)
    def _(c):
        weights(c).start()

    low, high = blocks - 1, 0
    for h in range(heads):
        for j in range(nv):
            v = vertical[h, j]
            inside = v - me * blocks
            mine = (inside >= 0) & (inside < blocks)
            low = jnp.minimum(low, jnp.where(mine, inside, blocks - 1))
            high = jnp.maximum(high, jnp.where(mine, inside, 0))
    inputs[0].wait()
    inputs[1].wait()
    for half, kv in enumerate((k_ref, v_ref)):
        at = slice(half * HS, (half + 1) * HS)
        window[reach:, :, at] = kv[...]
        pool[z, x, y, 0, :, at] = kv[low]
        pool[z, x, y, 1, :, at] = kv[high]

    pl.semaphore_wait(barrier, len(partners))

    def push(n, ref, to):
        return pltpu.make_async_remote_copy(
            src_ref=ref, dst_ref=ref, send_sem=g_send.at[n], recv_sem=g_recv.at[n],
            device_id=to, device_id_type=MESH,
        )

    def got(n, ref):
        push(n, ref, after).wait_recv()

    sent = []

    def send(n, ref, to):
        copy = push(n, ref, to)
        copy.start()
        sent.append(copy)

    up, down = (z + 1) % NZ, (z + NZ - 1) % NZ
    right, left = (y + 1) % NY, (y + NY - 1) % NY
    send(0, pool.at[z, x, y], mirror)
    near = pltpu.make_async_remote_copy(
        src_ref=window.at[pl.ds(reach, blocks)], dst_ref=window.at[pl.ds(reach - blocks, blocks)],
        send_sem=g_send.at[25], recv_sem=g_recv.at[25], device_id=after, device_id_type=MESH,
    )

    halves = (x, 1 - x)

    def first(k):
        for d in range(1, NY):
            send(6 * k + d, pool.at[z, halves[k], y, 0], ctx(z, x, y + d))
        for d in range(1, NZ):
            send(6 * k + 3 + d, pool.at[z, halves[k], y, 1], ctx(z + d, x, y))

    def second(k):
        for d in range(1, NY):
            got(6 * k + d, pool.at[z, halves[k], (y + NY - d) % NY, 0])
        send(13 + 4 * k, pool.at[z, halves[k], :, 0], ctx(z + 1, x, y))
        send(14 + 4 * k, pool.at[z, halves[k], :, 0], ctx(z + NZ - 1, x, y))
        for d in range(1, NZ):
            got(6 * k + 3 + d, pool.at[(z + NZ - d) % NZ, halves[k], y, 1])
        send(15 + 4 * k, pool.at[:, halves[k], y, 1], ctx(z, x, y + 1))
        send(16 + 4 * k, pool.at[:, halves[k], y, 1], ctx(z, x, y + NY - 1))

    first(0)
    got(0, pool.at[z, 1 - x, y])
    first(1)
    near.start()
    second(0)
    second(1)
    for copy in inputs[2:]:
        copy.wait()
    vert = vert_v[...]
    shard = vert >> (blocks.bit_length() - 1)
    start = vert & ~(blocks - 1)
    second = jnp.zeros((heads, nv), jnp.int32)
    for h in range(heads):
        for j in range(nv):
            v = vertical[h, j]
            second = jnp.where((start <= v) & (v < vert), 1, second)
    slots_v[...] = 2 * shard + second
    place = pltpu.make_async_copy(slots_v, slots, slot_sem)
    place.start()
    vert_wide = spread(vert, nv, BLK)
    slash_wide = spread(slash_v[...], ns, BLK)
    for i in range(blocks):
        block = me * blocks + i
        away = block - vert_wide
        kept = away > 0
        for j in range(ns):
            kept = kept & (away != slash_v[:, j : j + 1])
        bv[i] = jnp.where(kept, 0.0, NEG)
        bs[i] = jnp.where(slash_wide <= block, 0.0, NEG)

    near.wait_recv()
    far = pltpu.make_async_remote_copy(
        src_ref=window.at[pl.ds(reach - blocks + 1, blocks - 1)],
        dst_ref=window.at[pl.ds(reach - 2 * blocks + 1, blocks - 1)],
        send_sem=g_send.at[26], recv_sem=g_recv.at[26], device_id=after, device_id_type=MESH,
    )
    far.start()
    got(13, pool.at[down, x, :, 0])
    send(21, pool.at[down, x, :, 0], ctx(z + 1, x, y))
    got(15, pool.at[:, x, left, 1])
    send(23, pool.at[:, x, left, 1], ctx(z, x, y + 1))
    got(18, pool.at[up, 1 - x, :, 0])
    send(22, pool.at[up, 1 - x, :, 0], ctx(z + NZ - 1, x, y))
    got(20, pool.at[:, 1 - x, right, 1])
    send(24, pool.at[:, 1 - x, right, 1], ctx(z, x, y + NY - 1))
    got(16, pool.at[:, x, right, 1])
    got(19, pool.at[:, 1 - x, left, 1])
    got(14, pool.at[up, x, :, 0])
    got(17, pool.at[down, 1 - x, :, 0])
    got(21, pool.at[(z + 2) % NZ, x, :, 0])
    got(22, pool.at[(z + 2) % NZ, 1 - x, :, 0])
    got(23, pool.at[:, x, (y + 2) % NY, 1])
    got(24, pool.at[:, 1 - x, (y + 2) % NY, 1])
    far.wait_recv()
    place.wait()

    def hand(k, c):
        return pltpu.make_async_remote_copy(
            src_ref=to_sib.at[k, c],
            dst_ref=from_sib.at[k, c],
            send_sem=sib_send.at[k, c],
            recv_sem=sib_recv.at[k, c],
            device_id={"tp": sibling},
            device_id_type=MESH,
        )

    def over(half, c):
        to = {"tp": cross} if half == 0 else {**mirror, "tp": cross}
        return pltpu.make_async_remote_copy(
            src_ref=to_cross.at[c, half],
            dst_ref=from_cross.at[c, half],
            send_sem=cross_send.at[half, c],
            recv_sem=cross_recv.at[half, c],
            device_id=to,
            device_id_type=MESH,
        )

    def lend(n):
        at = pl.ds(pl.multiple_of(n * TOGETHER * HS, TOGETHER * HS), TOGETHER * HS)
        return pltpu.make_async_remote_copy(
            src_ref=att.at[0, :, :, at],
            dst_ref=att.at[2, :, :, at],
            send_sem=lend_send.at[n],
            recv_sem=lend_recv.at[n],
            device_id=mirror,
            device_id_type=MESH,
        )

    blocks_of_pool = pool.reshape(count * 2, BLK, 2 * HS)

    def attend(n, places, to):
        hs = [TOGETHER * n + k for k in range(TOGETHER)]
        attend_heads(hs, places, slots, slash, queries, blocks_of_pool, window, bv, bs, att, to)

    def project(parts, c):
        rows = jnp.concatenate([att[a, b] for a, b in parts], axis=0)
        return jnp.dot(rows, w[c], preferred_element_type=jnp.float32)

    @pl.loop(0, heads // TOGETHER)
    def _(n):
        places = (2 * corner + 1, 2 * cross + 1, 2 * corner, 2 * cross)
        attend(n, places, ((0, 0), (0, 1), (1, 0), (1, 1)))
        lend(n).start()

    def attend_here(n):
        places = (2 * sibling, 2 * sibling + 1, 2 * t, 2 * t + 1)
        attend(n, places, ((3, 0), (3, 1), (4, 0), (4, 1)))

    @pl.loop(0, AHEAD)
    def _(n):
        attend_here(n)

    for n in range(heads // TOGETHER):
        lend(n).wait_recv()

    def pass_on(c):
        hand(0, c).wait_recv()
        part = kept_back[c % BEHIND] + from_sib[0, c].astype(jnp.float32)
        for half in range(2):
            to_cross[c, half] = part[half * BLK : (half + 1) * BLK].astype(jnp.bfloat16)
            over(half, c).start()

    @pl.loop(0, chunks)
    def _(c):
        weights(c).wait()
        part = project(((1, 0), (2, 0), (1, 1), (2, 1)), c)
        to_sib[0, c] = part[: 2 * BLK].astype(jnp.bfloat16)
        hand(0, c).start()

        @pl.when(c >= BEHIND)
        def _():
            pass_on(c - BEHIND)

        kept_back[c % BEHIND] = part[2 * BLK :]

    @pl.loop(chunks - BEHIND, chunks)
    def _(c):
        pass_on(c)

    @pl.loop(AHEAD, heads // TOGETHER)
    def _(n):
        attend_here(n)

    @pl.loop(0, chunks)
    def _(c):
        part = project(((3, 0), (3, 1), (4, 0), (4, 1)), c)
        to_sib[1, c] = part[: 2 * BLK].astype(jnp.bfloat16)
        hand(1, c).start()
        held[c] = part[2 * BLK :]

    @pl.loop(0, chunks)
    def _(c):
        hand(1, c).wait_recv()
        part = held[c] + from_sib[1, c].astype(jnp.float32)
        at = pl.ds(pl.multiple_of(c * WIDE, WIDE), WIDE)
        for half in range(2):
            over(half, c).wait_recv()
            here = part[half * BLK : (half + 1) * BLK]
            out_ref[half * BLK : (half + 1) * BLK, at] = (
                here + from_cross[c, half].astype(jnp.float32)
            ).astype(jnp.bfloat16)

    @pl.loop(0, chunks)
    def _(c):
        hand(0, c).wait_send()
        hand(1, c).wait_send()
        over(0, c).wait_send()
        over(1, c).wait_send()

    for n in range(heads // TOGETHER):
        lend(n).wait_send()

    for copy in sent + [near, far]:
        copy.wait_send()


def shards(queries, keys, values, out_weight, vertical, slash):
    rows, width = queries.shape
    heads, nv = vertical.shape
    ns = slash.shape[1]
    blocks = rows // BLK
    chunks = out_weight.shape[1] // WIDE
    part = (rows // 4, WIDE)
    vmem = pl.BlockSpec(memory_space=pltpu.VMEM)
    smem = pl.BlockSpec(memory_space=pltpu.SMEM)
    dma = pltpu.SemaphoreType.DMA
    return pl.pallas_call(
        layer_kernel,
        out_shape=jax.ShapeDtypeStruct((rows // 4, out_weight.shape[1]), jnp.bfloat16),
        in_specs=[smem, smem] + [pl.BlockSpec(memory_space=pltpu.HBM)] * 6,
        out_specs=vmem,
        scratch_shapes=[
            pltpu.VMEM((blocks, BLK, HS), jnp.bfloat16),
            pltpu.VMEM((blocks, BLK, HS), jnp.bfloat16),
            pltpu.VMEM((heads, nv), jnp.int32),
            pltpu.VMEM((heads, ns), jnp.int32),
            pltpu.VMEM((blocks, BLK, width), jnp.bfloat16),
            pltpu.VMEM((NZ, NX, NY, 2, BLK, 2 * HS), jnp.bfloat16),
            pltpu.VMEM((3 * blocks, BLK, 2 * HS), jnp.bfloat16),
            pltpu.VMEM((blocks, heads, nv * BLK), jnp.float32),
            pltpu.VMEM((blocks, heads, ns * BLK), jnp.float32),
            pltpu.VMEM((heads, nv), jnp.int32),
            pltpu.SMEM((heads, nv), jnp.int32),
            pltpu.VMEM((5, 2, BLK, width), jnp.bfloat16),
            pltpu.VMEM((chunks, width, WIDE), jnp.bfloat16),
            pltpu.VMEM((2, chunks) + part, jnp.bfloat16),
            pltpu.VMEM((2, chunks) + part, jnp.bfloat16),
            pltpu.VMEM((chunks, 2, BLK, WIDE), jnp.bfloat16),
            pltpu.VMEM((chunks, 2, BLK, WIDE), jnp.bfloat16),
            pltpu.VMEM((BEHIND,) + part, jnp.float32),
            pltpu.VMEM((chunks,) + part, jnp.float32),
            dma((5,)),
            dma,
            dma((chunks,)),
            dma((2, chunks)),
            dma((2, chunks)),
            dma((2, chunks)),
            dma((2, chunks)),
            dma((heads // TOGETHER,)),
            dma((heads // TOGETHER,)),
            dma((27,)),
            dma((27,)),
        ],
        compiler_params=pltpu.CompilerParams(
            collective_id=0, has_side_effects=True, vmem_limit_bytes=60 << 20
        ),
    )(
        vertical, slash, vertical, slash, queries.reshape(blocks, BLK, width),
        keys.reshape(blocks, BLK, HS),
        values.reshape(blocks, BLK, HS), out_weight,
    )


def solution(mesh):
    return jax.shard_map(
        shards,
        mesh=mesh,
        in_specs=(
            P("ctx", "tp"),
            P("ctx", "tp"),
            P("ctx", "tp"),
            P("tp", None),
            P("tp", None),
            P("tp", None),
        ),
        out_specs=P(("ctx", "tp"), None),
        check_vma=False,
    )
```

```python
import jax
import jax.numpy as jnp
from jax import lax
from jax.experimental import pallas as pl
from jax.experimental.pallas import tpu as pltpu
from jax.sharding import PartitionSpec as P

HS = 128
BLK = 64
NEG = -1e30
MESH = pl.DeviceIdType.MESH
WIDE = 1024
NZ, NX, NY = 4, 2, 4
TOGETHER = 2
BEHIND = 3
AHEAD = 1


def attend_heads(hs, places, slots, slash, queries, pool, window, bv, bs, att, to):
    nv, ns = slots.shape[1], slash.shape[1]
    reach = window.shape[0] - queries.shape[0]
    scale = 1.4426950408889634 / (HS**0.5)
    over_keys = (((1,), (1,)), ((), ()))
    row = lax.broadcasted_iota(jnp.int32, (BLK, BLK), 0)
    col = lax.broadcasted_iota(jnp.int32, (BLK, BLK), 1)
    triangle = jnp.where(col > row, NEG, 0.0).astype(jnp.float32)
    lanes = [pl.ds(pl.multiple_of(h * HS, HS), HS) for h in hs]
    scores, v_vert, v_slash = [], [], []
    for h, lane in zip(hs, lanes):
        at_v = [slots[h, j] for j in range(nv)]
        k_vert = jnp.concatenate([pool[a, :, :HS] for a in at_v], axis=0)
        v_vert.append(jnp.concatenate([pool[a, :, HS:] for a in at_v], axis=0))
        q = jnp.concatenate([queries[i, :, lane] for i in places], axis=0)
        s_vert = lax.dot_general(q, k_vert, over_keys, preferred_element_type=jnp.float32)
        for n, i in enumerate(places):
            at = [reach + i - slash[h, j] for j in range(ns)]
            k_s = jnp.concatenate([window[a, :, :HS] for a in at], axis=0)
            v_slash.append(jnp.concatenate([window[a, :, HS:] for a in at], axis=0))
            rows = slice(n * BLK, (n + 1) * BLK)
            s_s = lax.dot_general(q[rows], k_s, over_keys, preferred_element_type=jnp.float32)
            scores.append((s_vert[rows], s_s, bv[i, pl.ds(h, 1), :], bs[i, pl.ds(h, 1), :]))
    weights, totals = [], []
    for s_v, s_s, b_v, b_s in scores:
        s_v = s_v + b_v
        s_s = jnp.concatenate([s_s[:, :BLK] + triangle, s_s[:, BLK:]], axis=1) + b_s
        m = jnp.maximum(jnp.max(s_v, axis=1, keepdims=True), jnp.max(s_s, axis=1, keepdims=True))
        w_v, w_s = jnp.exp2((s_v - m) * scale), jnp.exp2((s_s - m) * scale)
        totals.append(jnp.sum(w_v, axis=1, keepdims=True) + jnp.sum(w_s, axis=1, keepdims=True))
        weights.append((w_v.astype(jnp.bfloat16), w_s.astype(jnp.bfloat16)))
    for n, lane in enumerate(lanes):
        own = range(n * len(places), (n + 1) * len(places))
        o_v = jnp.dot(
            jnp.concatenate([weights[k][0] for k in own], axis=0), v_vert[n],
            preferred_element_type=jnp.float32,
        )
        for k, (slot, half) in zip(own, to):
            o_s = jnp.dot(weights[k][1], v_slash[k], preferred_element_type=jnp.float32)
            at = k - own[0]
            o = (o_v[at * BLK : (at + 1) * BLK] + o_s) / totals[k]
            att[slot, half, :, lane] = o.astype(jnp.bfloat16)


def spread(values, copies, width):
    lane = lax.broadcasted_iota(jnp.int32, (values.shape[0], copies * width), 1) // width
    out = jnp.zeros(lane.shape, jnp.int32)
    for j in range(copies):
        out = jnp.where(lane == j, values[:, j : j + 1], out)
    return out


def layer_kernel(
    vertical, slash, vert_hbm, slash_hbm, q_hbm, k_hbm, v_hbm, w_hbm, out_hbm,
    k_ref, v_ref, vert_v, slash_v, queries, pool, window, bv, bs, slots_v, slots, att, w,
    to_sib, from_sib, to_cross, from_cross, kept_back, held, done,
    done_sem, in_sem, slot_sem, w_sem, sib_send, sib_recv, cross_send, cross_recv,
    lend_send, lend_recv, g_send, g_recv,
):
    heads, nv = vertical.shape
    ns = slash.shape[1]
    chunks = w.shape[0]
    blocks = k_hbm.shape[0]
    reach = window.shape[0] - blocks
    t = lax.axis_index("tp")
    chip, core = t // 2, t % 2
    sibling = 2 * chip + (1 - core)
    cross = 2 * (1 - chip) + core
    corner = 2 * (1 - chip) + (1 - core)
    me = lax.axis_index("ctx")
    z, x, y = me // (NX * NY), (me // NY) % NX, me % NY
    count = NZ * NX * NY

    def ctx(zz, xx, yy):
        return {"ctx": (zz % NZ) * (NX * NY) + xx * NY + yy % NY}

    after, before = {"ctx": (me + 1) % count}, {"ctx": (me + count - 1) % count}
    barrier = pltpu.get_barrier_semaphore()
    mirror = ctx(z, 1 - x, y)
    partners = [{"tp": sibling}, {"tp": cross}, {**mirror, "tp": cross}, after, before, mirror]
    partners += [ctx(z, x, y + d) for d in range(1, NY)] + [ctx(z + d, x, y) for d in range(1, NZ)]
    for other in partners:
        pl.semaphore_signal(barrier, inc=1, device_id=other, device_id_type=MESH)

    def weights(c):
        at = pl.ds(pl.multiple_of(c * WIDE, WIDE), WIDE)
        return pltpu.make_async_copy(w_hbm.at[:, at], w.at[c], w_sem.at[c])

    inputs = [
        (k_hbm, k_ref),
        (v_hbm, v_ref),
        (vert_hbm, vert_v),
        (slash_hbm, slash_v),
        (q_hbm, queries),
    ]
    inputs = [pltpu.make_async_copy(a, b, in_sem.at[n]) for n, (a, b) in enumerate(inputs)]
    for copy in inputs:
        copy.start()

    @pl.loop(0, chunks)
    def _(c):
        weights(c).start()

    low, high = blocks - 1, 0
    for h in range(heads):
        for j in range(nv):
            v = vertical[h, j]
            inside = v - me * blocks
            mine = (inside >= 0) & (inside < blocks)
            low = jnp.minimum(low, jnp.where(mine, inside, blocks - 1))
            high = jnp.maximum(high, jnp.where(mine, inside, 0))
    inputs[0].wait()
    inputs[1].wait()
    for half, kv in enumerate((k_ref, v_ref)):
        at = slice(half * HS, (half + 1) * HS)
        window[reach:, :, at] = kv[...]
        pool[z, x, y, 0, :, at] = kv[low]
        pool[z, x, y, 1, :, at] = kv[high]

    pl.semaphore_wait(barrier, len(partners))

    def push(n, ref, to):
        return pltpu.make_async_remote_copy(
            src_ref=ref, dst_ref=ref, send_sem=g_send.at[n], recv_sem=g_recv.at[n],
            device_id=to, device_id_type=MESH,
        )

    def got(n, ref):
        push(n, ref, after).wait_recv()

    sent = []

    def send(n, ref, to):
        copy = push(n, ref, to)
        copy.start()
        sent.append(copy)

    up, down = (z + 1) % NZ, (z + NZ - 1) % NZ
    right, left = (y + 1) % NY, (y + NY - 1) % NY
    send(0, pool.at[z, x, y], mirror)
    near = pltpu.make_async_remote_copy(
        src_ref=window.at[pl.ds(reach, blocks)], dst_ref=window.at[pl.ds(reach - blocks, blocks)],
        send_sem=g_send.at[25], recv_sem=g_recv.at[25], device_id=after, device_id_type=MESH,
    )

    halves = (x, 1 - x)

    def first(k):
        for d in range(1, NY):
            send(6 * k + d, pool.at[z, halves[k], y, 0], ctx(z, x, y + d))
        for d in range(1, NZ):
            send(6 * k + 3 + d, pool.at[z, halves[k], y, 1], ctx(z + d, x, y))

    def second(k):
        for d in range(1, NY):
            got(6 * k + d, pool.at[z, halves[k], (y + NY - d) % NY, 0])
        send(13 + 4 * k, pool.at[z, halves[k], :, 0], ctx(z + 1, x, y))
        send(14 + 4 * k, pool.at[z, halves[k], :, 0], ctx(z + NZ - 1, x, y))
        for d in range(1, NZ):
            got(6 * k + 3 + d, pool.at[(z + NZ - d) % NZ, halves[k], y, 1])
        send(15 + 4 * k, pool.at[:, halves[k], y, 1], ctx(z, x, y + 1))
        send(16 + 4 * k, pool.at[:, halves[k], y, 1], ctx(z, x, y + NY - 1))

    first(0)
    near.start()
    got(0, pool.at[z, 1 - x, y])
    first(1)
    second(0)
    second(1)
    for copy in inputs[2:]:
        copy.wait()
    vert = vert_v[...]
    shard = vert >> (blocks.bit_length() - 1)
    start = vert & ~(blocks - 1)
    second = jnp.zeros((heads, nv), jnp.int32)
    for h in range(heads):
        for j in range(nv):
            v = vertical[h, j]
            second = jnp.where((start <= v) & (v < vert), 1, second)
    slots_v[...] = 2 * shard + second
    place = pltpu.make_async_copy(slots_v, slots, slot_sem)
    place.start()
    vert_wide = spread(vert, nv, BLK)
    slash_wide = spread(slash_v[...], ns, BLK)
    for i in range(blocks):
        block = me * blocks + i
        away = block - vert_wide
        kept = away > 0
        for j in range(ns):
            kept = kept & (away != slash_v[:, j : j + 1])
        bv[i] = jnp.where(kept, 0.0, NEG)
        bs[i] = jnp.where(slash_wide <= block, 0.0, NEG)

    near.wait_recv()
    far = pltpu.make_async_remote_copy(
        src_ref=window.at[pl.ds(reach - blocks + 1, blocks - 1)],
        dst_ref=window.at[pl.ds(reach - 2 * blocks + 1, blocks - 1)],
        send_sem=g_send.at[26], recv_sem=g_recv.at[26], device_id=after, device_id_type=MESH,
    )
    far.start()
    got(13, pool.at[down, x, :, 0])
    send(21, pool.at[down, x, :, 0], ctx(z + 1, x, y))
    got(15, pool.at[:, x, left, 1])
    send(23, pool.at[:, x, left, 1], ctx(z, x, y + 1))
    got(18, pool.at[up, 1 - x, :, 0])
    send(22, pool.at[up, 1 - x, :, 0], ctx(z + NZ - 1, x, y))
    got(20, pool.at[:, 1 - x, right, 1])
    send(24, pool.at[:, 1 - x, right, 1], ctx(z, x, y + NY - 1))
    got(16, pool.at[:, x, right, 1])
    got(19, pool.at[:, 1 - x, left, 1])
    got(14, pool.at[up, x, :, 0])
    got(17, pool.at[down, 1 - x, :, 0])
    got(21, pool.at[(z + 2) % NZ, x, :, 0])
    got(22, pool.at[(z + 2) % NZ, 1 - x, :, 0])
    got(23, pool.at[:, x, (y + 2) % NY, 1])
    got(24, pool.at[:, 1 - x, (y + 2) % NY, 1])
    far.wait_recv()
    place.wait()

    def hand(k, c):
        return pltpu.make_async_remote_copy(
            src_ref=to_sib.at[k, c],
            dst_ref=from_sib.at[k, c],
            send_sem=sib_send.at[k, c],
            recv_sem=sib_recv.at[k, c],
            device_id={"tp": sibling},
            device_id_type=MESH,
        )

    def over(half, c):
        to = {"tp": cross} if half == 0 else {**mirror, "tp": cross}
        return pltpu.make_async_remote_copy(
            src_ref=to_cross.at[c, half],
            dst_ref=from_cross.at[c, half],
            send_sem=cross_send.at[half, c],
            recv_sem=cross_recv.at[half, c],
            device_id=to,
            device_id_type=MESH,
        )

    def lend(n):
        at = pl.ds(pl.multiple_of(n * TOGETHER * HS, TOGETHER * HS), TOGETHER * HS)
        return pltpu.make_async_remote_copy(
            src_ref=att.at[0, :, :, at],
            dst_ref=att.at[2, :, :, at],
            send_sem=lend_send.at[n],
            recv_sem=lend_recv.at[n],
            device_id=mirror,
            device_id_type=MESH,
        )

    blocks_of_pool = pool.reshape(count * 2, BLK, 2 * HS)

    def attend(n, places, to):
        hs = [TOGETHER * n + k for k in range(TOGETHER)]
        attend_heads(hs, places, slots, slash, queries, blocks_of_pool, window, bv, bs, att, to)

    def finish(c):
        at = pl.ds(pl.multiple_of(c * WIDE, WIDE), WIDE)
        return pltpu.make_async_copy(done.at[c], out_hbm.at[:, at], done_sem.at[c])

    def project(parts, c):
        rows = jnp.concatenate([att[a, b] for a, b in parts], axis=0)
        return jnp.dot(rows, w[c], preferred_element_type=jnp.float32)

    @pl.loop(0, heads // TOGETHER)
    def _(n):
        places = (2 * corner + 1, 2 * cross + 1, 2 * corner, 2 * cross)
        attend(n, places, ((0, 0), (0, 1), (1, 0), (1, 1)))
        lend(n).start()

    def attend_here(n):
        places = (2 * sibling, 2 * sibling + 1, 2 * t, 2 * t + 1)
        attend(n, places, ((3, 0), (3, 1), (4, 0), (4, 1)))

    @pl.loop(0, AHEAD)
    def _(n):
        attend_here(n)

    for n in range(heads // TOGETHER):
        lend(n).wait_recv()

    def pass_on(c):
        hand(0, c).wait_recv()
        part = kept_back[c % BEHIND] + from_sib[0, c].astype(jnp.float32)
        for half in range(2):
            to_cross[c, half] = part[half * BLK : (half + 1) * BLK].astype(jnp.bfloat16)
            over(half, c).start()

    @pl.loop(0, chunks)
    def _(c):
        weights(c).wait()
        part = project(((1, 0), (2, 0), (1, 1), (2, 1)), c)
        to_sib[0, c] = part[: 2 * BLK].astype(jnp.bfloat16)
        hand(0, c).start()

        @pl.when(c >= BEHIND)
        def _():
            pass_on(c - BEHIND)

        kept_back[c % BEHIND] = part[2 * BLK :]

    @pl.loop(chunks - BEHIND, chunks)
    def _(c):
        pass_on(c)

    @pl.loop(AHEAD, heads // TOGETHER)
    def _(n):
        attend_here(n)

    @pl.loop(0, chunks)
    def _(c):
        part = project(((3, 0), (3, 1), (4, 0), (4, 1)), c)
        to_sib[1, c] = part[: 2 * BLK].astype(jnp.bfloat16)
        hand(1, c).start()
        held[c] = part[2 * BLK :]

    @pl.loop(0, chunks)
    def _(c):
        hand(1, c).wait_recv()
        part = held[c] + from_sib[1, c].astype(jnp.float32)
        for half in range(2):
            over(half, c).wait_recv()
            here = part[half * BLK : (half + 1) * BLK]
            done[c, half * BLK : (half + 1) * BLK] = (
                here + from_cross[c, half].astype(jnp.float32)
            ).astype(jnp.bfloat16)
        finish(c).start()

    @pl.loop(0, chunks)
    def _(c):
        hand(0, c).wait_send()
        hand(1, c).wait_send()
        finish(c).wait()
        over(0, c).wait_send()
        over(1, c).wait_send()

    for n in range(heads // TOGETHER):
        lend(n).wait_send()

    for copy in sent + [near, far]:
        copy.wait_send()


def shards(queries, keys, values, out_weight, vertical, slash):
    rows, width = queries.shape
    heads, nv = vertical.shape
    ns = slash.shape[1]
    blocks = rows // BLK
    chunks = out_weight.shape[1] // WIDE
    part = (rows // 4, WIDE)
    smem = pl.BlockSpec(memory_space=pltpu.SMEM)
    dma = pltpu.SemaphoreType.DMA
    return pl.pallas_call(
        layer_kernel,
        out_shape=jax.ShapeDtypeStruct((rows // 4, out_weight.shape[1]), jnp.bfloat16),
        in_specs=[smem, smem] + [pl.BlockSpec(memory_space=pltpu.HBM)] * 6,
        out_specs=pl.BlockSpec(memory_space=pltpu.HBM),
        scratch_shapes=[
            pltpu.VMEM((blocks, BLK, HS), jnp.bfloat16),
            pltpu.VMEM((blocks, BLK, HS), jnp.bfloat16),
            pltpu.VMEM((heads, nv), jnp.int32),
            pltpu.VMEM((heads, ns), jnp.int32),
            pltpu.VMEM((blocks, BLK, width), jnp.bfloat16),
            pltpu.VMEM((NZ, NX, NY, 2, BLK, 2 * HS), jnp.bfloat16),
            pltpu.VMEM((3 * blocks, BLK, 2 * HS), jnp.bfloat16),
            pltpu.VMEM((blocks, heads, nv * BLK), jnp.float32),
            pltpu.VMEM((blocks, heads, ns * BLK), jnp.float32),
            pltpu.VMEM((heads, nv), jnp.int32),
            pltpu.SMEM((heads, nv), jnp.int32),
            pltpu.VMEM((5, 2, BLK, width), jnp.bfloat16),
            pltpu.VMEM((chunks, width, WIDE), jnp.bfloat16),
            pltpu.VMEM((2, chunks) + part, jnp.bfloat16),
            pltpu.VMEM((2, chunks) + part, jnp.bfloat16),
            pltpu.VMEM((chunks, 2, BLK, WIDE), jnp.bfloat16),
            pltpu.VMEM((chunks, 2, BLK, WIDE), jnp.bfloat16),
            pltpu.VMEM((BEHIND,) + part, jnp.float32),
            pltpu.VMEM((chunks,) + part, jnp.float32),
            pltpu.VMEM((chunks,) + part, jnp.bfloat16),
            dma((chunks,)),
            dma((5,)),
            dma,
            dma((chunks,)),
            dma((2, chunks)),
            dma((2, chunks)),
            dma((2, chunks)),
            dma((2, chunks)),
            dma((heads // TOGETHER,)),
            dma((heads // TOGETHER,)),
            dma((27,)),
            dma((27,)),
        ],
        compiler_params=pltpu.CompilerParams(
            collective_id=0, has_side_effects=True, vmem_limit_bytes=60 << 20
        ),
    )(
        vertical, slash, vertical, slash, queries.reshape(blocks, BLK, width),
        keys.reshape(blocks, BLK, HS),
        values.reshape(blocks, BLK, HS), out_weight,
    )


def solution(mesh):
    return jax.shard_map(
        shards,
        mesh=mesh,
        in_specs=(
            P("ctx", "tp"),
            P("ctx", "tp"),
            P("ctx", "tp"),
            P("tp", None),
            P("tp", None),
            P("tp", None),
        ),
        out_specs=P(("ctx", "tp"), None),
        check_vma=False,
    )
```

```python
import jax
import jax.numpy as jnp
from jax import lax
from jax.experimental import pallas as pl
from jax.experimental.pallas import tpu as pltpu
from jax.sharding import PartitionSpec as P

HS = 128
BLK = 64
NEG = -1e30
MESH = pl.DeviceIdType.MESH
WIDE = 1024
NZ, NX, NY = 4, 2, 4
TOGETHER = 2
BEHIND = 3
AHEAD = 0


def attend_heads(hs, places, slots, slash, queries, pool, window, bv, bs, att, to):
    nv, ns = slots.shape[1], slash.shape[1]
    reach = window.shape[0] - queries.shape[0]
    scale = 1.4426950408889634 / (HS**0.5)
    over_keys = (((1,), (1,)), ((), ()))
    row = lax.broadcasted_iota(jnp.int32, (BLK, BLK), 0)
    col = lax.broadcasted_iota(jnp.int32, (BLK, BLK), 1)
    triangle = jnp.where(col > row, NEG, 0.0).astype(jnp.float32)
    lanes = [pl.ds(pl.multiple_of(h * HS, HS), HS) for h in hs]
    scores, v_vert, v_slash = [], [], []
    for h, lane in zip(hs, lanes):
        at_v = [slots[h, j] for j in range(nv)]
        k_vert = jnp.concatenate([pool[a, :, :HS] for a in at_v], axis=0)
        v_vert.append(jnp.concatenate([pool[a, :, HS:] for a in at_v], axis=0))
        q = jnp.concatenate([queries[i, :, lane] for i in places], axis=0)
        s_vert = lax.dot_general(q, k_vert, over_keys, preferred_element_type=jnp.float32)
        for n, i in enumerate(places):
            at = [reach + i - slash[h, j] for j in range(ns)]
            k_s = jnp.concatenate([window[a, :, :HS] for a in at], axis=0)
            v_slash.append(jnp.concatenate([window[a, :, HS:] for a in at], axis=0))
            rows = slice(n * BLK, (n + 1) * BLK)
            s_s = lax.dot_general(q[rows], k_s, over_keys, preferred_element_type=jnp.float32)
            scores.append((s_vert[rows], s_s, bv[i, pl.ds(h, 1), :], bs[i, pl.ds(h, 1), :]))
    weights, totals = [], []
    for s_v, s_s, b_v, b_s in scores:
        s_v = s_v + b_v
        s_s = jnp.concatenate([s_s[:, :BLK] + triangle, s_s[:, BLK:]], axis=1) + b_s
        m = jnp.maximum(jnp.max(s_v, axis=1, keepdims=True), jnp.max(s_s, axis=1, keepdims=True))
        w_v, w_s = jnp.exp2((s_v - m) * scale), jnp.exp2((s_s - m) * scale)
        totals.append(jnp.sum(w_v, axis=1, keepdims=True) + jnp.sum(w_s, axis=1, keepdims=True))
        weights.append((w_v.astype(jnp.bfloat16), w_s.astype(jnp.bfloat16)))
    for n, lane in enumerate(lanes):
        own = range(n * len(places), (n + 1) * len(places))
        o_v = jnp.dot(
            jnp.concatenate([weights[k][0] for k in own], axis=0), v_vert[n],
            preferred_element_type=jnp.float32,
        )
        for k, (slot, half) in zip(own, to):
            o_s = jnp.dot(weights[k][1], v_slash[k], preferred_element_type=jnp.float32)
            at = k - own[0]
            o = (o_v[at * BLK : (at + 1) * BLK] + o_s) / totals[k]
            att[slot, half, :, lane] = o.astype(jnp.bfloat16)


def spread(values, copies, width):
    lane = lax.broadcasted_iota(jnp.int32, (values.shape[0], copies * width), 1) // width
    out = jnp.zeros(lane.shape, jnp.int32)
    for j in range(copies):
        out = jnp.where(lane == j, values[:, j : j + 1], out)
    return out


def layer_kernel(
    vertical, slash, vert_hbm, slash_hbm, q_hbm, k_hbm, v_hbm, w_hbm, out_hbm,
    k_ref, v_ref, vert_v, slash_v, queries, pool, window, bv, bs, slots_v, slots, att, w,
    to_sib, from_sib, to_cross, from_cross, kept_back, held, done,
    done_sem, in_sem, slot_sem, w_sem, sib_send, sib_recv, cross_send, cross_recv,
    lend_send, lend_recv, g_send, g_recv,
):
    heads, nv = vertical.shape
    ns = slash.shape[1]
    chunks = w.shape[0]
    blocks = k_hbm.shape[0]
    reach = window.shape[0] - blocks
    t = lax.axis_index("tp")
    chip, core = t // 2, t % 2
    sibling = 2 * chip + (1 - core)
    cross = 2 * (1 - chip) + core
    corner = 2 * (1 - chip) + (1 - core)
    me = lax.axis_index("ctx")
    z, x, y = me // (NX * NY), (me // NY) % NX, me % NY
    count = NZ * NX * NY

    def ctx(zz, xx, yy):
        return {"ctx": (zz % NZ) * (NX * NY) + xx * NY + yy % NY}

    after, before = {"ctx": (me + 1) % count}, {"ctx": (me + count - 1) % count}
    barrier = pltpu.get_barrier_semaphore()
    mirror = ctx(z, 1 - x, y)
    partners = [{"tp": sibling}, {"tp": cross}, {**mirror, "tp": cross}, after, before, mirror]
    partners += [ctx(z, x, y + d) for d in range(1, NY)] + [ctx(z + d, x, y) for d in range(1, NZ)]
    for other in partners:
        pl.semaphore_signal(barrier, inc=1, device_id=other, device_id_type=MESH)

    def weights(c):
        at = pl.ds(pl.multiple_of(c * WIDE, WIDE), WIDE)
        return pltpu.make_async_copy(w_hbm.at[:, at], w.at[c], w_sem.at[c])

    inputs = [
        (k_hbm, k_ref),
        (v_hbm, v_ref),
        (vert_hbm, vert_v),
        (slash_hbm, slash_v),
        (q_hbm, queries),
    ]
    inputs = [pltpu.make_async_copy(a, b, in_sem.at[n]) for n, (a, b) in enumerate(inputs)]
    for copy in inputs:
        copy.start()

    @pl.loop(0, chunks)
    def _(c):
        weights(c).start()

    low, high = blocks - 1, 0
    for h in range(heads):
        for j in range(nv):
            v = vertical[h, j]
            inside = v - me * blocks
            mine = (inside >= 0) & (inside < blocks)
            low = jnp.minimum(low, jnp.where(mine, inside, blocks - 1))
            high = jnp.maximum(high, jnp.where(mine, inside, 0))
    inputs[0].wait()
    inputs[1].wait()
    for half, kv in enumerate((k_ref, v_ref)):
        at = slice(half * HS, (half + 1) * HS)
        window[reach:, :, at] = kv[...]
        pool[z, x, y, 0, :, at] = kv[low]
        pool[z, x, y, 1, :, at] = kv[high]

    pl.semaphore_wait(barrier, len(partners))

    def push(n, ref, to):
        return pltpu.make_async_remote_copy(
            src_ref=ref, dst_ref=ref, send_sem=g_send.at[n], recv_sem=g_recv.at[n],
            device_id=to, device_id_type=MESH,
        )

    def got(n, ref):
        push(n, ref, after).wait_recv()

    sent = []

    def send(n, ref, to):
        copy = push(n, ref, to)
        copy.start()
        sent.append(copy)

    up, down = (z + 1) % NZ, (z + NZ - 1) % NZ
    right, left = (y + 1) % NY, (y + NY - 1) % NY
    send(0, pool.at[z, x, y], mirror)
    near = pltpu.make_async_remote_copy(
        src_ref=window.at[pl.ds(reach, blocks)], dst_ref=window.at[pl.ds(reach - blocks, blocks)],
        send_sem=g_send.at[25], recv_sem=g_recv.at[25], device_id=after, device_id_type=MESH,
    )

    halves = (x, 1 - x)

    def first(k):
        for d in range(1, NY):
            send(6 * k + d, pool.at[z, halves[k], y, 0], ctx(z, x, y + d))
        for d in range(1, NZ):
            send(6 * k + 3 + d, pool.at[z, halves[k], y, 1], ctx(z + d, x, y))

    def second(k):
        for d in range(1, NY):
            got(6 * k + d, pool.at[z, halves[k], (y + NY - d) % NY, 0])
        send(13 + 4 * k, pool.at[z, halves[k], :, 0], ctx(z + 1, x, y))
        send(14 + 4 * k, pool.at[z, halves[k], :, 0], ctx(z + NZ - 1, x, y))
        for d in range(1, NZ):
            got(6 * k + 3 + d, pool.at[(z + NZ - d) % NZ, halves[k], y, 1])
        send(15 + 4 * k, pool.at[:, halves[k], y, 1], ctx(z, x, y + 1))
        send(16 + 4 * k, pool.at[:, halves[k], y, 1], ctx(z, x, y + NY - 1))

    first(0)
    near.start()
    got(0, pool.at[z, 1 - x, y])
    first(1)
    second(0)
    second(1)
    for copy in inputs[2:]:
        copy.wait()
    vert = vert_v[...]
    shard = vert >> (blocks.bit_length() - 1)
    start = vert & ~(blocks - 1)
    second = jnp.zeros((heads, nv), jnp.int32)
    for h in range(heads):
        for j in range(nv):
            v = vertical[h, j]
            second = jnp.where((start <= v) & (v < vert), 1, second)
    slots_v[...] = 2 * shard + second
    place = pltpu.make_async_copy(slots_v, slots, slot_sem)
    place.start()
    vert_wide = spread(vert, nv, BLK)
    slash_wide = spread(slash_v[...], ns, BLK)
    for i in range(blocks):
        block = me * blocks + i
        away = block - vert_wide
        kept = away > 0
        for j in range(ns):
            kept = kept & (away != slash_v[:, j : j + 1])
        bv[i] = jnp.where(kept, 0.0, NEG)
        bs[i] = jnp.where(slash_wide <= block, 0.0, NEG)

    near.wait_recv()
    far = pltpu.make_async_remote_copy(
        src_ref=window.at[pl.ds(reach - blocks + 1, blocks - 1)],
        dst_ref=window.at[pl.ds(reach - 2 * blocks + 1, blocks - 1)],
        send_sem=g_send.at[26], recv_sem=g_recv.at[26], device_id=after, device_id_type=MESH,
    )
    far.start()
    got(13, pool.at[down, x, :, 0])
    send(21, pool.at[down, x, :, 0], ctx(z + 1, x, y))
    got(15, pool.at[:, x, left, 1])
    send(23, pool.at[:, x, left, 1], ctx(z, x, y + 1))
    got(18, pool.at[up, 1 - x, :, 0])
    send(22, pool.at[up, 1 - x, :, 0], ctx(z + NZ - 1, x, y))
    got(20, pool.at[:, 1 - x, right, 1])
    send(24, pool.at[:, 1 - x, right, 1], ctx(z, x, y + NY - 1))
    got(16, pool.at[:, x, right, 1])
    got(19, pool.at[:, 1 - x, left, 1])
    got(14, pool.at[up, x, :, 0])
    got(17, pool.at[down, 1 - x, :, 0])
    got(21, pool.at[(z + 2) % NZ, x, :, 0])
    got(22, pool.at[(z + 2) % NZ, 1 - x, :, 0])
    got(23, pool.at[:, x, (y + 2) % NY, 1])
    got(24, pool.at[:, 1 - x, (y + 2) % NY, 1])
    far.wait_recv()
    place.wait()

    def hand(k, c):
        return pltpu.make_async_remote_copy(
            src_ref=to_sib.at[k, c],
            dst_ref=from_sib.at[k, c],
            send_sem=sib_send.at[k, c],
            recv_sem=sib_recv.at[k, c],
            device_id={"tp": sibling},
            device_id_type=MESH,
        )

    def over(half, c):
        to = {"tp": cross} if half == 0 else {**mirror, "tp": cross}
        return pltpu.make_async_remote_copy(
            src_ref=to_cross.at[c, half],
            dst_ref=from_cross.at[c, half],
            send_sem=cross_send.at[half, c],
            recv_sem=cross_recv.at[half, c],
            device_id=to,
            device_id_type=MESH,
        )

    def lend(n):
        at = pl.ds(pl.multiple_of(n * TOGETHER * HS, TOGETHER * HS), TOGETHER * HS)
        return pltpu.make_async_remote_copy(
            src_ref=att.at[0, :, :, at],
            dst_ref=att.at[2, :, :, at],
            send_sem=lend_send.at[n],
            recv_sem=lend_recv.at[n],
            device_id=mirror,
            device_id_type=MESH,
        )

    blocks_of_pool = pool.reshape(count * 2, BLK, 2 * HS)

    def attend(n, places, to):
        hs = [TOGETHER * n + k for k in range(TOGETHER)]
        attend_heads(hs, places, slots, slash, queries, blocks_of_pool, window, bv, bs, att, to)

    def finish(c):
        at = pl.ds(pl.multiple_of(c * WIDE, WIDE), WIDE)
        return pltpu.make_async_copy(done.at[c], out_hbm.at[:, at], done_sem.at[c])

    def project(parts, c):
        rows = jnp.concatenate([att[a, b] for a, b in parts], axis=0)
        return jnp.dot(rows, w[c], preferred_element_type=jnp.float32)

    @pl.loop(0, heads // TOGETHER)
    def _(n):
        places = (2 * corner + 1, 2 * cross + 1, 2 * corner, 2 * cross)
        attend(n, places, ((0, 0), (0, 1), (1, 0), (1, 1)))
        lend(n).start()

    def attend_here(n):
        places = (2 * sibling, 2 * sibling + 1, 2 * t, 2 * t + 1)
        attend(n, places, ((3, 0), (3, 1), (4, 0), (4, 1)))

    @pl.loop(0, AHEAD)
    def _(n):
        attend_here(n)

    for n in range(heads // TOGETHER):
        lend(n).wait_recv()

    def pass_on(c):
        hand(0, c).wait_recv()
        part = kept_back[c % BEHIND] + from_sib[0, c].astype(jnp.float32)
        for half in range(2):
            to_cross[c, half] = part[half * BLK : (half + 1) * BLK].astype(jnp.bfloat16)
            over(half, c).start()

    @pl.loop(0, chunks)
    def _(c):
        weights(c).wait()
        part = project(((1, 0), (2, 0), (1, 1), (2, 1)), c)
        to_sib[0, c] = part[: 2 * BLK].astype(jnp.bfloat16)
        hand(0, c).start()

        @pl.when(c >= BEHIND)
        def _():
            pass_on(c - BEHIND)

        kept_back[c % BEHIND] = part[2 * BLK :]

    @pl.loop(chunks - BEHIND, chunks)
    def _(c):
        pass_on(c)

    @pl.loop(AHEAD, heads // TOGETHER)
    def _(n):
        attend_here(n)

    @pl.loop(0, chunks)
    def _(c):
        part = project(((3, 0), (3, 1), (4, 0), (4, 1)), c)
        to_sib[1, c] = part[: 2 * BLK].astype(jnp.bfloat16)
        hand(1, c).start()
        held[c] = part[2 * BLK :]

    @pl.loop(0, chunks)
    def _(c):
        hand(1, c).wait_recv()
        part = held[c] + from_sib[1, c].astype(jnp.float32)
        for half in range(2):
            over(half, c).wait_recv()
            here = part[half * BLK : (half + 1) * BLK]
            done[c, half * BLK : (half + 1) * BLK] = (
                here + from_cross[c, half].astype(jnp.float32)
            ).astype(jnp.bfloat16)
        finish(c).start()

    @pl.loop(0, chunks)
    def _(c):
        hand(0, c).wait_send()
        hand(1, c).wait_send()
        finish(c).wait()
        over(0, c).wait_send()
        over(1, c).wait_send()

    for n in range(heads // TOGETHER):
        lend(n).wait_send()

    for copy in sent + [near, far]:
        copy.wait_send()


def shards(queries, keys, values, out_weight, vertical, slash):
    rows, width = queries.shape
    heads, nv = vertical.shape
    ns = slash.shape[1]
    blocks = rows // BLK
    chunks = out_weight.shape[1] // WIDE
    part = (rows // 4, WIDE)
    smem = pl.BlockSpec(memory_space=pltpu.SMEM)
    dma = pltpu.SemaphoreType.DMA
    return pl.pallas_call(
        layer_kernel,
        out_shape=jax.ShapeDtypeStruct((rows // 4, out_weight.shape[1]), jnp.bfloat16),
        in_specs=[smem, smem] + [pl.BlockSpec(memory_space=pltpu.HBM)] * 6,
        out_specs=pl.BlockSpec(memory_space=pltpu.HBM),
        scratch_shapes=[
            pltpu.VMEM((blocks, BLK, HS), jnp.bfloat16),
            pltpu.VMEM((blocks, BLK, HS), jnp.bfloat16),
            pltpu.VMEM((heads, nv), jnp.int32),
            pltpu.VMEM((heads, ns), jnp.int32),
            pltpu.VMEM((blocks, BLK, width), jnp.bfloat16),
            pltpu.VMEM((NZ, NX, NY, 2, BLK, 2 * HS), jnp.bfloat16),
            pltpu.VMEM((3 * blocks, BLK, 2 * HS), jnp.bfloat16),
            pltpu.VMEM((blocks, heads, nv * BLK), jnp.float32),
            pltpu.VMEM((blocks, heads, ns * BLK), jnp.float32),
            pltpu.VMEM((heads, nv), jnp.int32),
            pltpu.SMEM((heads, nv), jnp.int32),
            pltpu.VMEM((5, 2, BLK, width), jnp.bfloat16),
            pltpu.VMEM((chunks, width, WIDE), jnp.bfloat16),
            pltpu.VMEM((2, chunks) + part, jnp.bfloat16),
            pltpu.VMEM((2, chunks) + part, jnp.bfloat16),
            pltpu.VMEM((chunks, 2, BLK, WIDE), jnp.bfloat16),
            pltpu.VMEM((chunks, 2, BLK, WIDE), jnp.bfloat16),
            pltpu.VMEM((BEHIND,) + part, jnp.float32),
            pltpu.VMEM((chunks,) + part, jnp.float32),
            pltpu.VMEM((chunks,) + part, jnp.bfloat16),
            dma((chunks,)),
            dma((5,)),
            dma,
            dma((chunks,)),
            dma((2, chunks)),
            dma((2, chunks)),
            dma((2, chunks)),
            dma((2, chunks)),
            dma((heads // TOGETHER,)),
            dma((heads // TOGETHER,)),
            dma((27,)),
            dma((27,)),
        ],
        compiler_params=pltpu.CompilerParams(
            collective_id=0, has_side_effects=True, vmem_limit_bytes=60 << 20
        ),
    )(
        vertical, slash, vertical, slash, queries.reshape(blocks, BLK, width),
        keys.reshape(blocks, BLK, HS),
        values.reshape(blocks, BLK, HS), out_weight,
    )


def solution(mesh):
    return jax.shard_map(
        shards,
        mesh=mesh,
        in_specs=(
            P("ctx", "tp"),
            P("ctx", "tp"),
            P("ctx", "tp"),
            P("tp", None),
            P("tp", None),
            P("tp", None),
        ),
        out_specs=P(("ctx", "tp"), None),
        check_vma=False,
    )
```
